512 devices in a mesh: seq: 64 (over z, y), tp: 8 (over x, core).
Axes of the slice: x: 4, y: 8, z: 8, core: 2. Of those that a mesh axis runs over, the one named last changes fastest.
Arguments:
- tokens: bfloat16 [384, 2048], P('seq', 'tp'), may hold values from -6 to 6
- norm_gain: float32 [2048], replicated, may hold values from 0.25 to 4
- w_query: bfloat16 [2048, 2048], P(None, 'tp'), may hold values from -0.125 to 0.125
- w_key_value: bfloat16 [2, 2048, 1024], P(None, None, 'tp'), may hold values from -0.125 to 0.125
- w_out: bfloat16 [2048, 2048], P('tp'), may hold values from -0.125 to 0.125
- kv_pool: bfloat16 [2, 7168, 16, 1024], P(None, 'seq', None, 'tp'), may hold values from -256 to 256
- slot_owner: int32 [7168, 2], P('seq'), may hold values from -1 to 1791, as said below
- slot_dest: int32 [7168], P('seq'), may hold values from -1 to 7167, as said below
- lengths: int32 [96], replicated, may hold values from 1 to 28668, as said below
Outputs:
- attn_out: bfloat16 [384, 2048], P('seq', 'tp')
- kv_moved: bfloat16 [2, 7168, 16, 1024], P(None, 'seq', None, 'tp')
The draws below stay inside these ranges and needn't reach their ends.
Inputs may be any that keep to these rules, and one draw needn't show every extreme that they name: `lengths`: two requests are long, at least 22934 and one of them exactly 28668; the others hold at most 444. `slot_owner`: pages 0 to (lengths[r] + 3) // 16 of every request r are held by exactly one slot each, no other pages by any; a free slot holds (-1, -1). `slot_dest`: -1 where the page stays. Destinations are distinct, each a free slot or a slot whose own page moves. At most 2 slots of one index of seq move to slots of one index of seq, and exactly 2 do for some pair in every draw.
All inputs are finite; a program needn't handle non-finite values.
Results may differ from the reference program's by a relative error of at most 0.024.
The reference program's roundings to bfloat16 on the way (of `normed`, `queries`, `written` and `attended`) count: a program that leaves them out, or rounds other values in their place, can miss the bound.
Values may be sent and summed in bfloat16 or wider, within the bound.
A program may use at most 128 MiB of HBM per device.

```python
import math
import jax
import jax.numpy as jnp
from jax import lax

D = 2048
HEADS = 16
KV_HEADS = 8
HD = 128
STEPS = 4
PAGE = 16
SLOTS = 112
ROWS = 384
REQS = 96
LONG_MAX = 28668
LONG_MIN = 22934
SHORT_MAX = 444
N_SEQ = 64


def layout(key):
    base_key = jax.random.fold_in(key, 4242)
    pick_key, short_key, long_key, device_key = jax.random.split(base_key, 4)
    slot_total = N_SEQ * SLOTS
    chosen = jax.random.permutation(pick_key, REQS)
    first_long = jnp.minimum(chosen[0], chosen[1])
    second_long = jnp.maximum(chosen[0], chosen[1])
    lengths = jax.random.randint(short_key, (REQS,), 1, SHORT_MAX + 1)
    other_len = jax.random.randint(long_key, (), LONG_MIN, LONG_MAX + 1)
    flip_bit = jax.random.randint(jax.random.fold_in(long_key, 1), (), 0, 2)
    len_first = jnp.where(flip_bit == 0, LONG_MAX, other_len)
    len_second = jnp.where(flip_bit == 0, other_len, LONG_MAX)
    lengths = lengths.at[first_long].set(len_first).at[second_long].set(len_second)
    page_need = (lengths + STEPS - 1) // PAGE + 1
    request_ids = jnp.arange(REQS, dtype=jnp.int32)
    is_long = (request_ids == first_long) | (request_ids == second_long)
    pages_first = page_need[first_long]
    long_total = pages_first + page_need[second_long]
    devices = jax.random.permutation(device_key, N_SEQ)
    slot_major = jnp.arange(slot_total, dtype=jnp.int32)
    logical_dev = slot_major % N_SEQ
    logical_slot = slot_major // N_SEQ
    logical_index = logical_dev * SLOTS + logical_slot
    takes_long = logical_index < long_total
    short_rank = jnp.cumsum(jnp.where(takes_long, 0, 1)) - 1
    short_pages = jnp.where(is_long, 0, page_need)
    page_ends = jnp.cumsum(short_pages)
    short_req = jnp.minimum(jnp.searchsorted(page_ends, short_rank, side='right'), REQS - 1).astype(jnp.int32)
    short_page = short_rank - (page_ends[short_req] - short_pages[short_req])
    has_short = ~takes_long & (short_rank < page_ends[-1])
    long_req = jnp.where(logical_index < pages_first, first_long, second_long)
    long_page = jnp.where(logical_index < pages_first, logical_index, logical_index - pages_first)
    owner_req = jnp.where(takes_long, long_req, jnp.where(has_short, short_req, -1))
    owner_page = jnp.where(takes_long, long_page, jnp.where(has_short, short_page, -1))
    physical = devices[logical_dev] * SLOTS + logical_slot
    owner_table = jnp.full((slot_total, 2), -1, jnp.int32)
    owner_table = owner_table.at[physical].set(jnp.stack([owner_req, owner_page], axis=1).astype(jnp.int32))
    open_grid = (~has_short).reshape(SLOTS, N_SEQ).T
    open_rank = jnp.cumsum(open_grid.astype(jnp.int32), axis=1) - 1
    long_index = jnp.arange(slot_total, dtype=jnp.int32)
    target_dev = long_index % N_SEQ
    target_rank = long_index // N_SEQ
    matches = open_grid[target_dev] & (open_rank[target_dev] == target_rank[:, None])
    target_slot = jnp.argmax(matches.astype(jnp.int32), axis=1).astype(jnp.int32)
    dest_phys = devices[target_dev] * SLOTS + target_slot
    source_phys = devices[long_index // SLOTS] * SLOTS + long_index % SLOTS
    moved = long_index < long_total
    dest_table = jnp.full((slot_total,), -1, jnp.int32).at[source_phys].set(jnp.where(moved, dest_phys, -1).astype(jnp.int32))
    return (lengths.astype(jnp.int32), owner_table, dest_table)


def draw_lengths(key, part):
    return layout(key)[0]


def draw_slot_owner(key, part):
    return layout(key)[1]


def draw_slot_dest(key, part):
    return layout(key)[2]


def draw_kv_pool(key, part):
    pool_shape = (N_SEQ * SLOTS, PAGE, KV_HEADS * HD)
    key_part, value_part = jax.random.split(jax.random.fold_in(key, 515), 2)
    page_keys = 2.0 * jnp.clip(jax.random.normal(key_part, pool_shape), -4.0, 4.0)
    page_values = jnp.clip(jax.random.normal(value_part, pool_shape), -5.0, 5.0)
    return jnp.stack([page_keys, page_values]).astype(jnp.bfloat16)


def steps_of(own_key, extent, cuts, low, high):
    gain = 1.0
    for dim, blocks in cuts:
        heights = jax.random.uniform(jax.random.fold_in(jax.random.fold_in(own_key, 6), dim), (blocks,), jnp.float32, low / len(cuts), high / len(cuts))
        gain = gain * jnp.repeat(jnp.exp(heights), extent[dim] // blocks).reshape((-1,) + (1,) * (len(extent) - 1 - dim))
    return gain


def scatter_about(key, dims, deviation, reach, pieces=(), kind=jnp.bfloat16):
    drawn = deviation * jax.random.normal(key, dims, jnp.float32)
    if pieces:
        drawn = drawn * steps_of(key, dims, pieces, -0.22, 0.18)
    return jnp.clip(drawn, -reach, reach).astype(kind)


def setup_inputs(seed: int = 0) -> dict:
    keys = jax.random.split(jax.random.key(seed), 10)
    return {
        "tokens": scatter_about(keys[0], (ROWS, D), 1.0, 6.0, ((0, 64), (1, 8))),
        "norm_gain": jnp.clip(jnp.exp(jax.random.uniform(keys[1], (D,), jnp.float32, math.log(0.25), math.log(4.0))), 0.25, 4.0),
        "w_query": scatter_about(keys[2], (D, HEADS * HD), D ** -0.5, 0.125, ((1, 8),)),
        "w_key_value": scatter_about(keys[3], (2, D, KV_HEADS * HD), D ** -0.5, 0.125, ((2, 8),)),
        "w_out": scatter_about(keys[4], (HEADS * HD, D), (HEADS * HD) ** -0.5, 0.125, ((0, 8),)),
        "kv_pool": draw_kv_pool(jax.random.fold_in(keys[9], 71), 0),
        "slot_owner": draw_slot_owner(jax.random.fold_in(keys[9], 71), 0),
        "slot_dest": draw_slot_dest(jax.random.fold_in(keys[9], 71), 0),
        "lengths": draw_lengths(jax.random.fold_in(keys[9], 71), 0),
    }


ROPE_BASE = 1000000.0
NEG_FILL = -1e+30
NORM_EPS = 1e-06

def rotate(projected, positions, head_count):
    row_count = projected.shape[0]
    width = projected.shape[1] // head_count
    half_width = width // 2
    heads_view = projected.reshape(row_count, head_count, width)
    frequency = ROPE_BASE ** (-jnp.arange(half_width, dtype=jnp.float32) * 2.0 / width)
    angles = positions.astype(jnp.float32)[:, None] * frequency[None, :]
    cosine = jnp.cos(angles)[:, None, :]
    sine_part = jnp.sin(angles)[:, None, :]
    lower_half = heads_view[:, :, :half_width]
    upper_half = heads_view[:, :, half_width:]
    turned = jnp.concatenate([lower_half * cosine - upper_half * sine_part, upper_half * cosine + lower_half * sine_part], axis=2)
    return turned.reshape(row_count, head_count * width)

def reference(tokens, norm_gain, w_query, w_key_value, w_out, kv_pool, slot_owner, slot_dest, lengths):
    row_total = tokens.shape[0]
    row_index = jnp.arange(row_total, dtype=jnp.int32)
    positions = lengths[row_index // STEPS] + row_index % STEPS
    widened = tokens.astype(jnp.float32)
    mean_square = lax.optimization_barrier(jnp.mean(widened * widened, axis=1, keepdims=True))
    normed = (widened * lax.rsqrt(mean_square + NORM_EPS) * norm_gain.astype(jnp.float32)[None, :]).astype(jnp.bfloat16)
    queries = jnp.dot(normed, w_query, preferred_element_type=jnp.float32)
    key_proj = jnp.dot(normed, w_key_value[0], preferred_element_type=jnp.float32)
    value_proj = jnp.dot(normed, w_key_value[1], preferred_element_type=jnp.float32)
    queries = rotate(queries, positions, HEADS).astype(jnp.bfloat16)
    new_keys = rotate(key_proj, positions, KV_HEADS).astype(jnp.bfloat16)
    new_values = value_proj.astype(jnp.bfloat16)
    slot_total = kv_pool.shape[1]
    page_size = kv_pool.shape[2]
    owner_req = slot_owner[:, 0]
    owner_page = slot_owner[:, 1]
    occupied = owner_req >= 0
    safe_req = jnp.where(occupied, owner_req, 0)
    base_len = lengths[safe_req]
    offset = jnp.arange(page_size, dtype=jnp.int32)
    position = owner_page[:, None] * page_size + offset[None, :]
    step_of = position - base_len[:, None]
    is_new = occupied[:, None] & (step_of >= 0) & (step_of < STEPS)
    source_row = jnp.where(is_new, safe_req[:, None] * STEPS + step_of, 0).astype(jnp.int32)
    fresh_rows = jnp.stack([new_keys[source_row], new_values[source_row]])
    written = jnp.where(is_new[None, :, :, None], fresh_rows, kv_pool)
    group_size = HEADS // KV_HEADS
    step_ids = jnp.arange(STEPS, dtype=jnp.int32)
    visible = occupied[:, None, None] & (position[:, None, :] <= base_len[:, None, None] + step_ids[None, :, None])
    visible = visible[:, :, None, :]
    member = owner_req[None, :] == jnp.arange(REQS, dtype=jnp.int32)[:, None]
    segment = jnp.where(occupied, owner_req, REQS).astype(jnp.int32)
    slot_queries = queries.reshape(REQS, STEPS, KV_HEADS, group_size, HD)[safe_req]
    slot_queries = jnp.transpose(slot_queries, (2, 0, 1, 3, 4))
    page_keys = jnp.transpose(written[0].reshape(slot_total, page_size, KV_HEADS, HD), (2, 0, 1, 3))
    page_values = jnp.transpose(written[1].reshape(slot_total, page_size, KV_HEADS, HD), (2, 0, 1, 3))

    def one_head(head_parts):
        head_queries, head_keys, head_values = head_parts
        scores = jnp.einsum('stgd,spd->stgp', head_queries.astype(jnp.float32), head_keys.astype(jnp.float32)) * HD ** (-0.5)
        scores = jnp.where(visible, scores, NEG_FILL)
        slot_top = lax.optimization_barrier(jnp.max(scores, axis=3)).reshape(slot_total, -1)
        req_top = lax.optimization_barrier(jnp.max(jnp.where(member[:, :, None], slot_top[None, :, :], NEG_FILL), axis=1))
        slot_ref = req_top[safe_req].reshape(slot_total, STEPS, group_size, 1)
        weights = jnp.where(visible, jnp.exp(scores - slot_ref), 0.0)
        totals = jax.ops.segment_sum(lax.optimization_barrier(jnp.sum(weights, axis=3)), segment, num_segments=REQS + 1)[:REQS]
        rounded = lax.optimization_barrier(weights.astype(jnp.bfloat16)).astype(jnp.float32)
        products = jnp.einsum('stgp,spd->stgd', rounded, head_values.astype(jnp.float32))
        sums = jax.ops.segment_sum(products, segment, num_segments=REQS + 1)[:REQS]
        return sums / totals[..., None]
    per_head = lax.map(one_head, (slot_queries, page_keys, page_values))
    attended = jnp.transpose(per_head, (1, 2, 0, 3, 4)).reshape(row_total, HEADS * HD).astype(jnp.bfloat16)
    attn_out = jnp.dot(attended, w_out, preferred_element_type=jnp.float32).astype(jnp.bfloat16)
    moving = slot_dest >= 0
    slot_ids = jnp.arange(slot_total, dtype=jnp.int32)
    source_for = jnp.full((slot_total,), -1, jnp.int32).at[jnp.where(moving, slot_dest, slot_total)].set(slot_ids, mode='drop')
    landed = source_for >= 0
    incoming = written[:, jnp.where(landed, source_for, 0)]
    kv_moved = jnp.where(landed[None, :, None, None], incoming, jnp.where(moving[None, :, None, None], jnp.zeros_like(written), written))
    return (attn_out, kv_moved)
```

```python
import functools

import jax
import jax.numpy as jnp
from jax import lax
from jax.experimental import pallas as pl
from jax.experimental.pallas import tpu as pltpu
from jax.sharding import PartitionSpec as P

HD = 128
STEPS = 4
PADDED = 8
ROPE_BASE = 1000000.0
NEG_FILL = -1e30
NORM_EPS = 1e-06
VMEM = pltpu.VMEM
SMEM = pltpu.SMEM


def in_vmem():
    return pl.BlockSpec(memory_space=VMEM)


def in_smem():
    return pl.BlockSpec(memory_space=SMEM)


def take(table, index):
    ids = jnp.arange(table.shape[0], dtype=jnp.int32)
    return jnp.sum(jnp.where(index[:, None] == ids[None, :], table[None, :], 0), axis=1)


def rotate(projected, positions, head_count):
    row_count = projected.shape[0]
    width = projected.shape[1] // head_count
    half_width = width // 2
    heads_view = projected.reshape(row_count, head_count, width)
    frequency = ROPE_BASE ** (-jnp.arange(half_width, dtype=jnp.float32) * 2.0 / width)
    angles = positions.astype(jnp.float32)[:, None] * frequency[None, :]
    cosine = jnp.cos(angles)[:, None, :]
    sine_part = jnp.sin(angles)[:, None, :]
    lower_half = heads_view[:, :, :half_width]
    upper_half = heads_view[:, :, half_width:]
    turned = jnp.concatenate(
        [
            lower_half * cosine - upper_half * sine_part,
            upper_half * cosine + lower_half * sine_part,
        ],
        axis=2,
    )
    return turned.reshape(row_count, head_count * width)


def project_rows(token_block, norm_gain, w_query, w_key_value, positions):
    widened = token_block.astype(jnp.float32)
    mean_square = jnp.mean(widened * widened, axis=1, keepdims=True)
    normed = (widened * lax.rsqrt(mean_square + NORM_EPS) * norm_gain[None, :]).astype(jnp.bfloat16)
    queries = jnp.dot(normed, w_query, preferred_element_type=jnp.float32)
    keys = jnp.dot(normed, w_key_value[0], preferred_element_type=jnp.float32)
    values = jnp.dot(normed, w_key_value[1], preferred_element_type=jnp.float32)
    queries = rotate(queries, positions, w_query.shape[1] // HD).astype(jnp.bfloat16)
    fresh_key = rotate(keys, positions, w_key_value.shape[2] // HD).astype(jnp.bfloat16)
    return jnp.concatenate([queries, fresh_key, values.astype(jnp.bfloat16)], axis=1)


def pick_kernel(source_ref, pool_ref, out_ref):
    @pl.loop(0, out_ref.shape[0])
    def _(b):
        s = source_ref[b]
        out_ref[b, 0] = pool_ref[0, s]
        out_ref[b, 1] = pool_ref[1, s]


def overlay(base, source, fresh_all):
    rows = base.shape[0]
    ids = lax.broadcasted_iota(jnp.int32, (rows, fresh_all.shape[0]), 1)
    hot = jnp.where(ids == source, 1.0, 0.0).astype(jnp.bfloat16)
    fresh = jnp.dot(hot, fresh_all, preferred_element_type=jnp.float32)
    return jnp.where(source >= 0, fresh, base.astype(jnp.float32)).astype(jnp.bfloat16)


def attend_kernel(
    packed_ref, pool_ref, source_ref, owner_ref, pos_ref, req_ref, limit_ref, meta_ref,
    out_ref, keys, values,
):
    slots, page = pool_ref.shape[1], pool_ref.shape[2]
    entries = slots * page
    chunk_slots = 16
    chunk = chunk_slots * page

    @pl.loop(0, slots // chunk_slots)
    def _(c):
        at = pl.ds(pl.multiple_of(c * chunk, chunk), chunk)
        source = source_ref[at, :]
        for half, into in ((0, keys), (1, values)):
            base = pool_ref[half, pl.ds(c * chunk_slots, chunk_slots)].reshape(chunk, HD)
            fresh_all = packed_ref[:, (2 + half) * HD : (3 + half) * HD]
            into[at, :] = overlay(base, source, fresh_all)

    block = 64

    @pl.loop(0, packed_ref.shape[0] // block)
    def _(b):
        at = pl.ds(pl.multiple_of(b * block, block), block)
        visible = (owner_ref[...] == req_ref[at, :]) & (pos_ref[...] <= limit_ref[at, :])
        lane = lax.broadcasted_iota(jnp.int32, (block, HD), 1)
        stats = meta_ref[at, :]
        for g in range(2):
            query = packed_ref[at, g * HD : (g + 1) * HD]
            scores = lax.dot_general(
                query, keys[...], (((1,), (1,)), ((), ())), preferred_element_type=jnp.float32
            ) * HD ** (-0.5)
            scores = jnp.where(visible, scores, NEG_FILL)
            top = jnp.max(scores, axis=1, keepdims=True)
            weights = jnp.where(visible, jnp.exp(scores - top), 0.0)
            total = jnp.sum(weights, axis=1, keepdims=True)
            out_ref[at, g * HD : (g + 1) * HD] = jnp.dot(
                weights.astype(jnp.bfloat16), values[...], preferred_element_type=jnp.float32
            )
            stats = jnp.where(lane == g, top, jnp.where(lane == 2 + g, total, stats))
        out_ref[at, 2 * HD : 3 * HD] = stats


def place_kernel(from_ref, arrived_ref, pool_ref, source_ref, packed_ref, out_ref, base):
    slots, page = pool_ref.shape[1], pool_ref.shape[2]

    @pl.loop(0, slots)
    def _(g):
        s = from_ref[g]

        @pl.when(s >= 0)
        def _():
            base[0, g] = arrived_ref[s, 0]
            base[1, g] = arrived_ref[s, 1]

        @pl.when(s == -1)
        def _():
            base[0, g] = pool_ref[0, g]
            base[1, g] = pool_ref[1, g]

        @pl.when(s < -1)
        def _():
            base[0, g] = jnp.zeros_like(base[0, g])
            base[1, g] = jnp.zeros_like(base[1, g])

    chunk_slots = 16
    chunk = chunk_slots * page

    @pl.loop(0, slots // chunk_slots)
    def _(c):
        source = source_ref[pl.ds(pl.multiple_of(c * chunk, chunk), chunk), :]
        for half in range(2):
            at = pl.ds(c * chunk_slots, chunk_slots)
            fresh_all = packed_ref[:, (2 + half) * HD : (3 + half) * HD]
            out_ref[half, at] = overlay(
                base[half, at].reshape(chunk, HD), source, fresh_all
            ).reshape(chunk_slots, page, HD)


def new_sources(req, page, lengths, page_size, own_rows):
    base_len = take(lengths, req)
    offset = jnp.arange(page_size, dtype=jnp.int32)
    position = page[:, None] * page_size + offset[None, :]
    step_of = position - base_len[:, None]
    is_new = (req >= 0)[:, None] & (step_of >= 0) & (step_of < STEPS)
    row = req[:, None] * STEPS + step_of
    padded_row = row // own_rows * PADDED + row % own_rows
    return position, jnp.where(is_new, padded_row, -1)


def local(tokens, norm_gain, w_query, w_key_value, w_out, kv_pool, slot_owner, slot_dest, lengths):
    seq_count = lax.axis_size("seq")
    my_index = lax.axis_index("seq")
    own_rows = tokens.shape[0]
    slot_count = kv_pool.shape[1]
    page_size = kv_pool.shape[2]
    entries = slot_count * page_size
    capacity = -(-slot_count // seq_count)
    i32 = jnp.int32

    moving = slot_dest >= 0
    target_dev = jnp.where(moving, slot_dest // slot_count, -1)
    slot_ids = jnp.arange(slot_count, dtype=i32)
    same = (target_dev[None, :] == target_dev[:, None]) & (slot_ids[None, :] < slot_ids[:, None])
    send_rank = jnp.sum(same.astype(i32), axis=1)
    buffer_slot = jnp.where(moving, target_dev * capacity + send_rank, -1)
    hot = buffer_slot[None, :] == jnp.arange(seq_count * capacity, dtype=i32)[:, None]
    filled = jnp.any(hot, axis=1)

    def picked(values):
        return jnp.sum(jnp.where(hot, values[None, :], 0), axis=1)

    pick_slot = picked(slot_ids)
    outgoing = pl.pallas_call(
        pick_kernel,
        out_shape=jax.ShapeDtypeStruct(
            (seq_count * capacity, 2, page_size, HD), jnp.bfloat16
        ),
        in_specs=[in_smem(), in_vmem()],
        out_specs=in_vmem(),
        name="pick_pages",
    )(pick_slot, kv_pool)
    arrived = lax.all_to_all(outgoing, "seq", split_axis=0, concat_axis=0, tiled=True)
    meta = jnp.stack(
        [
            jnp.where(filled, picked(slot_dest % slot_count), -1),
            picked(slot_owner[:, 0]),
            picked(slot_owner[:, 1]),
        ],
        axis=1,
    ).astype(jnp.float32)
    meta = meta.reshape(seq_count, 1, capacity * 3)
    meta = jnp.pad(meta, ((0, 0), (0, 0), (4, HD - 4 - capacity * 3)))
    meta = jnp.broadcast_to(meta, (seq_count, PADDED, HD)).reshape(seq_count * PADDED, HD)

    own_tokens = lax.all_gather(tokens, "tp", axis=1, tiled=True)
    own_tokens = jnp.pad(own_tokens, ((0, PADDED - own_rows), (0, 0)))
    own_index = my_index * own_rows + jnp.arange(PADDED, dtype=i32)
    own_positions = take(lengths, own_index // STEPS) + own_index % STEPS
    own_packed = project_rows(own_tokens, norm_gain, w_query, w_key_value, own_positions)
    packed = lax.all_gather(own_packed[None], "seq", axis=0, tiled=True)
    packed = packed.reshape(seq_count * PADDED, own_packed.shape[1])

    padded_ids = jnp.arange(seq_count * PADDED, dtype=i32)
    row_of = padded_ids // PADDED * own_rows + padded_ids % PADDED
    real = padded_ids % PADDED < own_rows
    row_req = jnp.where(real, row_of // STEPS, -2)
    row_limit = take(lengths, row_req) + row_of % STEPS
    position, source = new_sources(
        slot_owner[:, 0], slot_owner[:, 1], lengths, page_size, own_rows
    )
    entry_owner = jnp.broadcast_to(slot_owner[:, :1], (slot_count, page_size))

    partials = pl.pallas_call(
        attend_kernel,
        out_shape=jax.ShapeDtypeStruct((seq_count * PADDED, 3 * HD), jnp.float32),
        in_specs=[in_vmem()] * 8,
        out_specs=in_vmem(),
        scratch_shapes=[VMEM((entries, HD), jnp.bfloat16)] * 2,
        name="attend",
    )(
        packed,
        kv_pool,
        source.reshape(entries, 1),
        entry_owner.reshape(1, entries),
        position.reshape(1, entries),
        row_req[:, None],
        row_limit[:, None],
        meta,
    )
    gathered = lax.all_to_all(
        partials.reshape(seq_count, PADDED, 3 * HD), "seq", split_axis=0, concat_axis=0, tiled=True
    )
    stats = gathered[:, :, 2 * HD :]
    top = stats[:, :, 0:2]
    peak = jnp.max(top, axis=0, keepdims=True)
    rescale = jnp.exp(top - peak)
    total = jnp.sum(stats[:, :, 2:4] * rescale, axis=0)
    summed = jnp.sum(gathered[:, :, : 2 * HD] * jnp.repeat(rescale, HD, axis=2), axis=0)
    total = jnp.where(total > 0.0, total, 1.0)
    attended = (summed / jnp.repeat(total, HD, axis=1)).astype(jnp.bfloat16)
    partial_out = jnp.dot(attended, w_out, preferred_element_type=jnp.float32)
    attn_out = lax.psum_scatter(
        partial_out[:own_rows].astype(jnp.bfloat16), "tp", scatter_dimension=1, tiled=True
    )

    came = stats[:, 0, 4 : 4 + capacity * 3].astype(i32).reshape(seq_count * capacity, 3)
    lands = came[None, :, 0] == slot_ids[:, None]
    landed = jnp.any(lands, axis=1)

    def landing(values):
        return jnp.sum(jnp.where(lands, values[None, :], 0), axis=1)

    stay_or_zero = jnp.where(moving, -2, -1)
    from_index = jnp.where(
        landed, landing(jnp.arange(seq_count * capacity, dtype=i32)), stay_or_zero
    )
    final_req = jnp.where(landed, landing(came[:, 1]), jnp.where(moving, -1, slot_owner[:, 0]))
    final_page = jnp.where(landed, landing(came[:, 2]), slot_owner[:, 1])
    _, final_source = new_sources(final_req, final_page, lengths, page_size, own_rows)
    kv_moved = pl.pallas_call(
        place_kernel,
        out_shape=jax.ShapeDtypeStruct(kv_pool.shape, kv_pool.dtype),
        in_specs=[in_smem()] + [in_vmem()] * 4,
        out_specs=in_vmem(),
        scratch_shapes=[VMEM(kv_pool.shape, kv_pool.dtype)],
        name="place_pages",
    )(from_index, arrived, kv_pool, final_source.reshape(entries, 1), packed)
    return (attn_out, kv_moved)


def solution(mesh):
    in_specs = (
        P("seq", "tp"),
        P(),
        P(None, "tp"),
        P(None, None, "tp"),
        P("tp", None),
        P(None, "seq", None, "tp"),
        P("seq", None),
        P("seq"),
        P(),
    )
    out_specs = (P("seq", "tp"), P(None, "seq", None, "tp"))
    return jax.shard_map(local, mesh=mesh, in_specs=in_specs, out_specs=out_specs, check_vma=False)
```

```python
import functools

import jax
import jax.numpy as jnp
from jax import lax
from jax.experimental import pallas as pl
from jax.experimental.pallas import tpu as pltpu
from jax.sharding import PartitionSpec as P

HD = 128
STEPS = 4
PADDED = 8
ROPE_BASE = 1000000.0
NEG_FILL = -1e30
NORM_EPS = 1e-06
VMEM = pltpu.VMEM
SMEM = pltpu.SMEM


def in_vmem():
    return pl.BlockSpec(memory_space=VMEM)


def in_smem():
    return pl.BlockSpec(memory_space=SMEM)


def take(table, index):
    ids = jnp.arange(table.shape[0], dtype=jnp.int32)
    return jnp.sum(jnp.where(index[:, None] == ids[None, :], table[None, :], 0), axis=1)


MESH = pl.DeviceIdType.MESH
EARLY = 24


def remote(source, into, send_sem, recv_sem, **where):
    return pltpu.make_async_remote_copy(
        src_ref=source,
        dst_ref=into,
        send_sem=send_sem,
        recv_sem=recv_sem,
        device_id=where,
        device_id_type=MESH,
    )


def split(value):
    first = value.astype(jnp.bfloat16).astype(jnp.float32)
    rest = value - first
    second = rest.astype(jnp.bfloat16).astype(jnp.float32)
    return first, second, rest - second


def block_kernel(
    pick_ref, tokens_ref, gain_ref, wq_ref, wkv_ref, wout_ref, cos_ref, sin_ref, pool_ref,
    source_ref, owner_ref, pos_ref, req_ref, limit_ref, meta_ref,
    out_ref, arrived_ref, came_ref, fresh_ref,
    tok, pkq, pkkv, queries, fresh_all, keys, values, outgoing, csend, crecv, rsend, rrecv,
    tok_s, tok_r, q1_s, q1_r, q2_s, q2_r, k1_s, k1_r, k2_s, k2_r,
    page_s, page_r, c_s, c_r, r_s, r_r,
):
    me = lax.axis_index("seq")
    tp = lax.axis_index("tp")
    y, z = lax.rem(me, 8), lax.div(me, 8)
    n_seq, n_tp = 64, 8
    slots, page = pool_ref.shape[1], pool_ref.shape[2]

    barrier = pltpu.get_barrier_semaphore()
    for k in range(1, n_tp):
        pl.semaphore_signal(
            barrier, inc=1, device_id={"tp": lax.rem(tp + k, n_tp)}, device_id_type=MESH
        )

    @pl.loop(1, n_seq)
    def _(k):
        pl.semaphore_signal(
            barrier, inc=1, device_id={"seq": lax.rem(me + k, n_seq)}, device_id_type=MESH
        )

    @pl.loop(0, n_seq)
    def _(d):
        for i in range(2):
            s = pick_ref[d * 2 + i]
            outgoing[d, i, 0] = pool_ref[0, s]
            outgoing[d, i, 1] = pool_ref[1, s]

    pl.semaphore_wait(barrier, n_seq - 1 + n_tp - 1)

    def token_copy(k):
        return remote(
            tokens_ref, tok.at[tp], tok_s.at[k], tok_r.at[k], tp=lax.rem(tp + k, n_tp)
        )

    for k in range(1, n_tp):
        token_copy(k).start()
    tok[tp] = tokens_ref[...]

    def page_copy(k):
        d = lax.rem(me + k, n_seq)
        return remote(outgoing.at[d], arrived_ref.at[me], page_s.at[k], page_r.at[k], seq=d)

    @pl.loop(1, 1 + EARLY)
    def _(k):
        page_copy(k).start()

    arrived_ref[me] = outgoing[me]

    for k in range(1, n_tp):
        token_copy(k).wait()

    square = jnp.zeros((PADDED, 1), jnp.float32)
    for i in range(n_tp):
        x = tok[i].astype(jnp.float32)
        square = square + jnp.sum(x * x, axis=1, keepdims=True)
    width = tok.shape[2]
    scale = lax.rsqrt(square / (n_tp * width) + NORM_EPS)
    q = jnp.zeros((PADDED, 2 * HD), jnp.float32)
    kk = jnp.zeros((PADDED, HD), jnp.float32)
    vv = jnp.zeros((PADDED, HD), jnp.float32)
    for i in range(n_tp):
        at = slice(i * width, (i + 1) * width)
        normed = (tok[i].astype(jnp.float32) * scale * gain_ref[i : i + 1, :]).astype(jnp.bfloat16)
        q = q + jnp.dot(normed, wq_ref[at, :], preferred_element_type=jnp.float32)
        kk = kk + jnp.dot(normed, wkv_ref[0, at, :], preferred_element_type=jnp.float32)
        vv = vv + jnp.dot(normed, wkv_ref[1, at, :], preferred_element_type=jnp.float32)

    def turn(x):
        return x * cos_ref[...] + pltpu.roll(x, HD // 2, 1) * sin_ref[...]

    pkq[z, y, :, 0:HD] = turn(q[:, 0:HD]).astype(jnp.bfloat16)
    pkq[z, y, :, HD : 2 * HD] = turn(q[:, HD : 2 * HD]).astype(jnp.bfloat16)
    pkkv[z, y, :, 0:HD] = turn(kk).astype(jnp.bfloat16)
    pkkv[z, y, :, HD : 2 * HD] = vv.astype(jnp.bfloat16)

    def along_y(k):
        return z * 8 + lax.rem(y + k, 8)

    def along_z(k):
        return lax.rem(z + k, 8) * 8 + y

    def q1(k):
        return remote(pkq.at[z, y], pkq.at[z, y], q1_s.at[k], q1_r.at[k], seq=along_y(k))

    def k1(k):
        return remote(pkkv.at[z, y], pkkv.at[z, y], k1_s.at[k], k1_r.at[k], seq=along_z(k))

    def q2(k):
        return remote(pkq.at[z], pkq.at[z], q2_s.at[k], q2_r.at[k], seq=along_z(k))

    def k2(k):
        return remote(pkkv.at[:, y], pkkv.at[:, y], k2_s.at[k], k2_r.at[k], seq=along_y(k))

    for k in range(1, 8):
        q1(k).start()
        k1(k).start()
    for k in range(1, 8):
        q1(k).wait()
    for k in range(1, 8):
        q2(k).start()
    for k in range(1, 8):
        k1(k).wait()
    for k in range(1, 8):
        k2(k).start()

    @pl.loop(1 + EARLY, n_seq)
    def _(k):
        page_copy(k).start()

    for k in range(1, 8):
        k2(k).wait()
    fresh = pkkv[...].astype(jnp.float32).reshape(n_seq * PADDED, 2 * HD)
    fresh_ref[...] = fresh.reshape(n_seq, PADDED, 2 * HD)
    fresh_all[...] = fresh.astype(jnp.bfloat16)

    chunk_slots = 16
    chunk = chunk_slots * page

    @pl.loop(0, slots // chunk_slots)
    def _(c):
        at = pl.ds(pl.multiple_of(c * chunk, chunk), chunk)
        source = source_ref[at, :]
        ids = lax.broadcasted_iota(jnp.int32, (chunk, n_seq * PADDED), 1)
        hot = jnp.where(ids == source, 1.0, 0.0).astype(jnp.bfloat16)
        new = jnp.dot(hot, fresh_all[...], preferred_element_type=jnp.float32)
        for half, into in ((0, keys), (1, values)):
            base = pool_ref[half, pl.ds(c * chunk_slots, chunk_slots)].reshape(chunk, HD)
            into[at, :] = jnp.where(
                source >= 0, new[:, half * HD : (half + 1) * HD], base.astype(jnp.float32)
            ).astype(jnp.bfloat16)

    for k in range(1, 8):
        q2(k).wait()
    queries[...] = (
        pkq[...].astype(jnp.float32).reshape(n_seq * PADDED, 2 * HD).astype(jnp.bfloat16)
    )

    def part_copy(d):
        return remote(csend.at[d], crecv.at[me], c_s.at[d], c_r.at[me], seq=d)

    block = 64

    @pl.loop(0, 8)
    def _(i):
        b = lax.rem(z + i, 8)
        at = pl.ds(pl.multiple_of(b * block, block), block)
        dests = pl.ds(b * 8, 8)
        visible = (owner_ref[...] == req_ref[at, :]) & (pos_ref[...] <= limit_ref[at, :])
        lane = lax.broadcasted_iota(jnp.int32, (block, HD), 1)
        stats = meta_ref[dests].reshape(block, HD)
        for g in range(2):
            query = queries[at, g * HD : (g + 1) * HD]
            scores = lax.dot_general(
                query, keys[...], (((1,), (1,)), ((), ())), preferred_element_type=jnp.float32
            ) * HD ** (-0.5)
            scores = jnp.where(visible, scores, NEG_FILL)
            top = jnp.max(scores, axis=1, keepdims=True)
            some = jnp.where(top > 0.5 * NEG_FILL, 1.0, 0.0)
            weights = jnp.exp(scores - top)
            total = jnp.sum(weights, axis=1, keepdims=True) * some
            part = some * jnp.dot(
                weights.astype(jnp.bfloat16), values[...], preferred_element_type=jnp.float32
            )
            csend[dests, :, g * HD : (g + 1) * HD] = part.reshape(8, PADDED, HD).astype(jnp.bfloat16)
            for j, piece in enumerate(split(top) + split(total)):
                stats = jnp.where(lane == 6 * g + j, piece, stats)
        csend[dests, :, 2 * HD : 3 * HD] = stats.reshape(8, PADDED, HD).astype(jnp.bfloat16)

        @pl.loop(0, 8)
        def _(j):
            d = b * 8 + j

            @pl.when(d != me)
            def _():
                part_copy(d).start()

    crecv[me] = csend[me]

    @pl.loop(0, n_seq)
    def _(d):
        @pl.when(d != me)
        def _():
            remote(csend.at[d], crecv.at[d], c_s.at[d], c_r.at[d], seq=d).wait()

    stats = crecv[:, :, 2 * HD : 3 * HD].astype(jnp.float32)
    came_ref[...] = stats
    mixed = []
    for g in range(2):
        def piece(j):
            return stats[:, :, j : j + 1] + stats[:, :, j + 1 : j + 2] + stats[:, :, j + 2 : j + 3]

        top = piece(6 * g)
        peak = jnp.max(top, axis=0, keepdims=True)
        rescale = jnp.exp(top - peak)
        total = jnp.sum(piece(6 * g + 3) * rescale, axis=0)
        part = crecv[:, :, g * HD : (g + 1) * HD].astype(jnp.float32)
        summed = jnp.sum(part * rescale, axis=0)
        total = jnp.where(total > 0.0, total, 1.0)
        mixed.append((summed / total).astype(jnp.bfloat16))
    attended = jnp.concatenate(mixed, axis=1)

    def sum_copy(k):
        to = lax.rem(tp + k, n_tp)
        return remote(rsend.at[to], rrecv.at[tp], r_s.at[k], r_r.at[k], tp=to)

    for i in range(n_tp):
        rsend[i] = jnp.dot(
            attended, wout_ref[:, i * width : (i + 1) * width], preferred_element_type=jnp.float32
        ).astype(jnp.bfloat16)
    for k in range(1, n_tp):
        sum_copy(k).start()
    rrecv[tp] = rsend[tp]
    for k in range(1, n_tp):
        sum_copy(k).wait()
    result = jnp.zeros((PADDED, width), jnp.float32)
    for i in range(n_tp):
        result = result + rrecv[i].astype(jnp.float32)
    out_ref[...] = result.astype(jnp.bfloat16)

    @pl.loop(1, n_seq)
    def _(k):
        page_copy(k).wait()


def place_kernel(from_ref, req_ref, start_ref, arrived_ref, pool_ref, fresh_ref, out_ref):
    slots, page = pool_ref.shape[1], pool_ref.shape[2]

    @pl.loop(0, slots)
    def _(g):
        s = from_ref[g]

        @pl.when(s >= 0)
        def _():
            out_ref[0, g] = arrived_ref[s, 0]
            out_ref[1, g] = arrived_ref[s, 1]

        @pl.when(s == -1)
        def _():
            out_ref[0, g] = pool_ref[0, g]
            out_ref[1, g] = pool_ref[1, g]

        @pl.when(s < -1)
        def _():
            out_ref[0, g] = jnp.zeros((page, HD), out_ref.dtype)
            out_ref[1, g] = jnp.zeros((page, HD), out_ref.dtype)

        start = start_ref[g]

        @pl.when((start > -STEPS) & (start < page))
        def _():
            ids = lax.broadcasted_iota(jnp.int32, (page, HD), 0)
            both = [out_ref[c, g].astype(jnp.float32) for c in range(2)]
            for t in range(STEPS):
                row = req_ref[g] * STEPS + t
                block = fresh_ref[lax.div(row, 6)]
                line = lax.broadcasted_iota(jnp.int32, block.shape, 0) == lax.rem(row, 6)
                entry = jnp.sum(jnp.where(line, block, 0.0), axis=0, keepdims=True)
                for c in range(2):
                    new = entry[:, c * HD : (c + 1) * HD]
                    both[c] = jnp.where(ids == start + t, new, both[c])
            for c in range(2):
                out_ref[c, g] = both[c].astype(out_ref.dtype)


def local(tokens, norm_gain, w_query, w_key_value, w_out, kv_pool, slot_owner, slot_dest, lengths):
    seq_count = lax.axis_size("seq")
    tp_count = lax.axis_size("tp")
    my_index = lax.axis_index("seq")
    own_rows = tokens.shape[0]
    width = tokens.shape[1]
    slot_count = kv_pool.shape[1]
    page_size = kv_pool.shape[2]
    entries = slot_count * page_size
    capacity = -(-slot_count // seq_count)
    i32 = jnp.int32
    f32 = jnp.float32
    bf16 = jnp.bfloat16

    moving = slot_dest >= 0
    target_dev = jnp.where(moving, slot_dest // slot_count, -1)
    slot_ids = jnp.arange(slot_count, dtype=i32)
    same = (target_dev[None, :] == target_dev[:, None]) & (slot_ids[None, :] < slot_ids[:, None])
    send_rank = jnp.sum(same.astype(i32), axis=1)
    buffer_slot = jnp.where(moving, target_dev * capacity + send_rank, -1)
    hot = buffer_slot[None, :] == jnp.arange(seq_count * capacity, dtype=i32)[:, None]
    filled = jnp.any(hot, axis=1)

    def picked(values):
        return jnp.sum(jnp.where(hot, values[None, :], 0), axis=1)

    pick_slot = picked(slot_ids)
    owner_req = slot_owner[:, 0]
    owner_page = slot_owner[:, 1]
    sent_page = picked(owner_page)
    meta = jnp.stack(
        [
            jnp.where(filled, picked(slot_dest % slot_count), -1),
            picked(owner_req),
            sent_page // 128,
            sent_page % 128,
        ],
        axis=1,
    ).astype(f32)
    meta = meta.reshape(seq_count, 1, capacity * 4)
    meta = jnp.pad(meta, ((0, 0), (0, 0), (12, HD - 12 - capacity * 4)))
    meta = jnp.broadcast_to(meta, (seq_count, PADDED, HD))

    own_index = my_index * own_rows + jnp.arange(PADDED, dtype=i32)
    own_positions = take(lengths, own_index // STEPS) + own_index % STEPS
    frequency = ROPE_BASE ** (-jnp.arange(HD // 2, dtype=f32) * 2.0 / HD)
    angles = own_positions.astype(f32)[:, None] * frequency[None, :]
    cosine, sine = jnp.cos(angles), jnp.sin(angles)
    cosine = jnp.concatenate([cosine, cosine], axis=1)
    sine = jnp.concatenate([-sine, sine], axis=1)

    padded_ids = jnp.arange(seq_count * PADDED, dtype=i32)
    row_of = padded_ids // PADDED * own_rows + padded_ids % PADDED
    real = padded_ids % PADDED < own_rows
    row_req = jnp.where(real, row_of // STEPS, -2)
    row_limit = take(lengths, row_req) + row_of % STEPS
    base_len = take(lengths, owner_req)
    offset = jnp.arange(page_size, dtype=i32)
    position = owner_page[:, None] * page_size + offset[None, :]
    step_of = position - base_len[:, None]
    is_new = (owner_req >= 0)[:, None] & (step_of >= 0) & (step_of < STEPS)
    row = owner_req[:, None] * STEPS + step_of
    source = jnp.where(is_new, row // own_rows * PADDED + row % own_rows, -1)
    entry_owner = jnp.broadcast_to(owner_req[:, None], (slot_count, page_size))

    rows = seq_count * PADDED
    page_shape = (seq_count, capacity, 2, page_size, HD)
    dma = pltpu.SemaphoreType.DMA
    attn_out, arrived, came, fresh = pl.pallas_call(
        block_kernel,
        out_shape=[
            jax.ShapeDtypeStruct((PADDED, width), bf16),
            jax.ShapeDtypeStruct(page_shape, bf16),
            jax.ShapeDtypeStruct((seq_count, PADDED, HD), f32),
            jax.ShapeDtypeStruct((seq_count, PADDED, 2 * HD), f32),
        ],
        in_specs=[in_smem()] + [in_vmem()] * 14,
        out_specs=[in_vmem()] * 4,
        scratch_shapes=[
            VMEM((tp_count, PADDED, width), bf16),
            VMEM((8, 8, PADDED, 2 * HD), bf16),
            VMEM((8, 8, PADDED, 2 * HD), bf16),
            VMEM((rows, 2 * HD), bf16),
            VMEM((rows, 2 * HD), bf16),
            VMEM((entries, HD), bf16),
            VMEM((entries, HD), bf16),
            VMEM(page_shape, bf16),
            VMEM((seq_count, PADDED, 3 * HD), bf16),
            VMEM((seq_count, PADDED, 3 * HD), bf16),
            VMEM((tp_count, PADDED, width), bf16),
            VMEM((tp_count, PADDED, width), bf16),
        ]
        + [dma((8,))] * 10
        + [dma((seq_count,))] * 4
        + [dma((8,))] * 2,
        compiler_params=pltpu.CompilerParams(collective_id=0, has_side_effects=True),
        name="block",
    )(
        pick_slot,
        jnp.pad(tokens, ((0, PADDED - own_rows), (0, 0))),
        norm_gain.reshape(tp_count, width),
        w_query,
        w_key_value,
        w_out,
        cosine,
        sine,
        kv_pool,
        source.reshape(entries, 1),
        entry_owner.reshape(1, entries),
        position.reshape(1, entries),
        row_req[:, None],
        row_limit[:, None],
        meta,
    )

    came = came[:, 0, 12 : 12 + capacity * 4].astype(i32).reshape(seq_count * capacity, 4)
    lands = came[None, :, 0] == slot_ids[:, None]
    landed = jnp.any(lands, axis=1)

    def landing(values):
        return jnp.sum(jnp.where(lands, values[None, :], 0), axis=1)

    from_index = jnp.where(
        landed,
        landing(jnp.arange(seq_count * capacity, dtype=i32)),
        jnp.where(moving, -2, -1),
    )
    came_req = came[:, 1]
    came_start = take(lengths, came_req) - (came[:, 2] * 128 + came[:, 3]) * page_size
    own_start = jnp.where(
        (owner_req < 0) | moving, page_size, base_len - owner_page * page_size
    )
    final_req = jnp.where(landed, landing(came_req), owner_req)
    final_start = jnp.where(landed, landing(came_start), own_start)
    kv_moved = pl.pallas_call(
        place_kernel,
        out_shape=jax.ShapeDtypeStruct(kv_pool.shape, kv_pool.dtype),
        in_specs=[in_smem()] * 3 + [in_vmem()] * 3,
        out_specs=in_vmem(),
        name="place_pages",
    )(
        from_index,
        final_req,
        final_start,
        arrived.reshape(seq_count * capacity, 2, page_size, HD),
        kv_pool,
        fresh,
    )
    return (attn_out[:own_rows], kv_moved)


def solution(mesh):
    in_specs = (
        P("seq", "tp"),
        P(),
        P(None, "tp"),
        P(None, None, "tp"),
        P("tp", None),
        P(None, "seq", None, "tp"),
        P("seq", None),
        P("seq"),
        P(),
    )
    out_specs = (P("seq", "tp"), P(None, "seq", None, "tp"))
    return jax.shard_map(local, mesh=mesh, in_specs=in_specs, out_specs=out_specs, check_vma=False)
```

```python
import functools

import jax
import jax.numpy as jnp
from jax import lax
from jax.experimental import pallas as pl
from jax.experimental.pallas import tpu as pltpu
from jax.sharding import PartitionSpec as P

HD = 128
STEPS = 4
PADDED = 8
ROPE_BASE = 1000000.0
NEG_FILL = -1e30
NORM_EPS = 1e-06
VMEM = pltpu.VMEM
SMEM = pltpu.SMEM


def in_vmem():
    return pl.BlockSpec(memory_space=VMEM)


def in_smem():
    return pl.BlockSpec(memory_space=SMEM)


def take(table, index):
    ids = jnp.arange(table.shape[0], dtype=jnp.int32)
    return jnp.sum(jnp.where(index[:, None] == ids[None, :], table[None, :], 0), axis=1)


MESH = pl.DeviceIdType.MESH
EARLY = 24


def remote(source, into, send_sem, recv_sem, **where):
    return pltpu.make_async_remote_copy(
        src_ref=source,
        dst_ref=into,
        send_sem=send_sem,
        recv_sem=recv_sem,
        device_id=where,
        device_id_type=MESH,
    )


def split(value):
    first = value.astype(jnp.bfloat16).astype(jnp.float32)
    rest = value - first
    second = rest.astype(jnp.bfloat16).astype(jnp.float32)
    return first, second, rest - second


def iota(shape, dim):
    return lax.broadcasted_iota(jnp.int32, shape, dim)


def ones_where(mask):
    return jnp.where(mask, 1.0, 0.0)


def prepare(
    owner_ref, dest_ref, lengths_ref, hot, entry_owner, entry_pos, req_ref, limit_ref, meta_ref,
    n_seq, slots, page, own_rows,
):
    f32, bf16 = jnp.float32, jnp.bfloat16
    rows, entries = n_seq * PADDED, slots * page
    across = (((1,), (1,)), ((), ()))
    owner = owner_ref[...].astype(f32)
    req, number = owner[0:1, :], owner[1:2, :]
    high = jnp.floor(number * (1.0 / 128))
    low = number - high * 128.0
    line = iota((HD, slots), 0)
    parts = jnp.where(line == 0, req, jnp.where(line == 1, high, jnp.where(line == 2, low, 0.0)))
    parts = parts.astype(bf16)

    spread = ones_where(
        lax.shift_right_logical(iota((slots, entries), 1), 4) == iota((slots, entries), 0)
    ).astype(bf16)
    wide = jnp.dot(parts[0:16, :], spread, preferred_element_type=f32)
    entry_owner[...] = wide[0:1, :]
    inner = (iota((1, entries), 1) & (page - 1)).astype(f32)
    entry_pos[...] = (wide[1:2, :] * 128.0 + wide[2:3, :]) * page + inner

    def row_facts(ids):
        j = ids & (PADDED - 1)
        row = lax.shift_right_logical(ids, 3) * own_rows + j
        wanted = jnp.where(j < own_rows, lax.shift_right_logical(row, 2), -2)
        return wanted.astype(f32), (row & (STEPS - 1)).astype(f32)

    lengths = lengths_ref[...].astype(f32)
    count = lengths.shape[1]
    wanted, step = row_facts(iota((rows, 1), 0))
    match = iota((rows, count), 1).astype(f32) == wanted
    req_ref[...] = wanted
    limit_ref[...] = step + jnp.sum(jnp.where(match, lengths, 0.0), axis=1, keepdims=True)
    eye = iota((count, count), 0) == iota((count, count), 1)
    length_col = jnp.sum(jnp.where(eye, lengths, 0.0), axis=1, keepdims=True)
    wanted_row, step_row = row_facts(iota((1, rows), 1))
    match = iota((count, rows), 0).astype(f32) == wanted_row
    limit_row = step_row + jnp.sum(jnp.where(match, length_col, 0.0), axis=0, keepdims=True)

    chunk = 16 * page

    @pl.loop(0, entries // chunk)
    def _(c):
        slot = lax.shift_right_logical(iota((chunk, slots), 0), 4) + c * 16
        near = ones_where(slot == iota((chunk, slots), 1)).astype(bf16)
        tall = lax.dot_general(near, parts, across, preferred_element_type=f32)
        at_inner = (iota((chunk, 1), 0) & (page - 1)).astype(f32)
        place = (tall[:, 1:2] * 128.0 + tall[:, 2:3]) * page + at_inner
        mask = (tall[:, 0:1] == wanted_row) & (place == limit_row)
        hot[pl.ds(pl.multiple_of(c * chunk, chunk), chunk), :] = ones_where(mask).astype(bf16)

    dest = dest_ref[...].astype(f32)
    device = jnp.floor((dest + 0.5) * (1.0 / slots))
    landing = dest - device * slots
    ahead, behind = iota((slots, slots), 0), iota((slots, slots), 1)
    device_col = jnp.sum(jnp.where(ahead == behind, device, 0.0), axis=1, keepdims=True)
    rank = jnp.sum(
        ones_where((device_col == device) & (ahead < behind)), axis=0, keepdims=True
    )
    place = jnp.where(dest >= 0.0, device * 2.0 + rank, -1.0)
    ids = iota((rows, slots), 0)
    j = ids & (PADDED - 1)
    wants = jnp.where(j < 2, lax.shift_right_logical(ids, 3) * 2 + j, -2).astype(f32)
    facts = jnp.where(
        line == 12,
        landing + 1.0,
        jnp.where(line == 13, req, jnp.where(line == 14, high, jnp.where(line == 15, low, 0.0))),
    )
    meta_ref[...] = lax.dot_general(
        ones_where(wants == place).astype(bf16),
        facts.astype(bf16),
        across,
        preferred_element_type=f32,
    )


def block_kernel(
    pick_ref, tokens_ref, gain_ref, wq_ref, wkv_ref, wout_ref, cos_ref, sin_ref, pool_ref,
    owner_ref, dest_ref, lengths_ref,
    out_ref, arrived_ref, came_ref, fresh_ref,
    tsend, hot, entry_owner, entry_pos, req_ref, limit_ref, meta_ref,
    tok, pkq, pkkv, queries, fresh_all, keys, values, outgoing, csend, crecv, rsend, rrecv,
    tok_s, tok_r, q1_s, q1_r, q2_s, q2_r, k1_s, k1_r, k2_s, k2_r,
    page_s, page_r, c_s, c_r, r_s, r_r,
):
    me = lax.axis_index("seq")
    tp = lax.axis_index("tp")
    y, z = lax.rem(me, 8), lax.div(me, 8)
    n_seq, n_tp = 64, 8
    slots, page = pool_ref.shape[1], pool_ref.shape[2]

    barrier = pltpu.get_barrier_semaphore()
    for k in range(1, n_tp):
        pl.semaphore_signal(
            barrier, inc=1, device_id={"tp": lax.rem(tp + k, n_tp)}, device_id_type=MESH
        )

    @pl.loop(1, n_seq)
    def _(k):
        pl.semaphore_signal(
            barrier, inc=1, device_id={"seq": lax.rem(me + k, n_seq)}, device_id_type=MESH
        )

    tsend[...] = jnp.zeros_like(tsend)
    tsend[0 : tokens_ref.shape[0], :] = tokens_ref[...]

    @pl.loop(0, n_seq)
    def _(d):
        for i in range(2):
            s = pick_ref[d * 2 + i]
            outgoing[d, i, 0] = pool_ref[0, s]
            outgoing[d, i, 1] = pool_ref[1, s]

    prepare(
        owner_ref, dest_ref, lengths_ref, hot, entry_owner, entry_pos, req_ref, limit_ref,
        meta_ref, n_seq, slots, page, tokens_ref.shape[0],
    )
    pl.semaphore_wait(barrier, n_seq - 1 + n_tp - 1)

    def token_copy(k):
        return remote(
            tsend, tok.at[tp], tok_s.at[k], tok_r.at[k], tp=lax.rem(tp + k, n_tp)
        )

    for k in range(1, n_tp):
        token_copy(k).start()
    tok[tp] = tsend[...]

    def page_copy(k):
        turn_by = lax.rem(k * 27, n_seq)
        d = lax.rem(z + lax.div(turn_by, 8), 8) * 8 + lax.rem(y + lax.rem(turn_by, 8), 8)
        return remote(outgoing.at[d], arrived_ref.at[me], page_s.at[k], page_r.at[k], seq=d)

    @pl.loop(1, 1 + EARLY)
    def _(k):
        page_copy(k).start()

    arrived_ref[me] = outgoing[me]

    for k in range(1, n_tp):
        token_copy(k).wait()

    square = jnp.zeros((PADDED, 1), jnp.float32)
    for i in range(n_tp):
        x = tok[i].astype(jnp.float32)
        square = square + jnp.sum(x * x, axis=1, keepdims=True)
    width = tok.shape[2]
    scale = lax.rsqrt(square / (n_tp * width) + NORM_EPS)
    q = jnp.zeros((PADDED, 2 * HD), jnp.float32)
    kk = jnp.zeros((PADDED, HD), jnp.float32)
    vv = jnp.zeros((PADDED, HD), jnp.float32)
    for i in range(n_tp):
        at = slice(i * width, (i + 1) * width)
        normed = (tok[i].astype(jnp.float32) * scale * gain_ref[:, at]).astype(jnp.bfloat16)
        q = q + jnp.dot(normed, wq_ref[at, :], preferred_element_type=jnp.float32)
        kk = kk + jnp.dot(normed, wkv_ref[0, at, :], preferred_element_type=jnp.float32)
        vv = vv + jnp.dot(normed, wkv_ref[1, at, :], preferred_element_type=jnp.float32)

    def turn(x):
        return x * cos_ref[...] + pltpu.roll(x, HD // 2, 1) * sin_ref[...]

    pkq[z, y, :, 0:HD] = turn(q[:, 0:HD]).astype(jnp.bfloat16)
    pkq[z, y, :, HD : 2 * HD] = turn(q[:, HD : 2 * HD]).astype(jnp.bfloat16)
    pkkv[z, y, :, 0:HD] = turn(kk).astype(jnp.bfloat16)
    pkkv[z, y, :, HD : 2 * HD] = vv.astype(jnp.bfloat16)

    def along_y(k):
        return z * 8 + lax.rem(y + k, 8)

    def along_z(k):
        return lax.rem(z + k, 8) * 8 + y

    def q1(k):
        return remote(pkq.at[z, y], pkq.at[z, y], q1_s.at[k], q1_r.at[k], seq=along_y(k))

    def k1(k):
        return remote(pkkv.at[z, y], pkkv.at[z, y], k1_s.at[k], k1_r.at[k], seq=along_z(k))

    def q2(k):
        return remote(pkq.at[z], pkq.at[z], q2_s.at[k], q2_r.at[k], seq=along_z(k))

    def k2(k):
        return remote(pkkv.at[:, y], pkkv.at[:, y], k2_s.at[k], k2_r.at[k], seq=along_y(k))

    for k in range(1, 8):
        q1(k).start()
        k1(k).start()
    for k in range(1, 8):
        q1(k).wait()
    for k in range(1, 8):
        q2(k).start()
    for k in range(1, 8):
        k1(k).wait()
    for k in range(1, 8):
        k2(k).start()

    @pl.loop(1 + EARLY, n_seq)
    def _(k):
        page_copy(k).start()

    for k in range(1, 8):
        k2(k).wait()
    fresh = pkkv[...].astype(jnp.float32).reshape(n_seq * PADDED, 2 * HD)
    fresh_ref[...] = fresh.reshape(n_seq, PADDED, 2 * HD)
    fresh_all[:, 0 : 2 * HD] = fresh.astype(jnp.bfloat16)
    fresh_all[:, 2 * HD : 3 * HD] = jnp.ones((n_seq * PADDED, HD), jnp.bfloat16)

    chunk_slots = 16
    chunk = chunk_slots * page

    @pl.loop(0, slots // chunk_slots)
    def _(c):
        at = pl.ds(pl.multiple_of(c * chunk, chunk), chunk)
        new = jnp.dot(hot[at, :], fresh_all[...], preferred_element_type=jnp.float32)
        is_new = new[:, 2 * HD : 3 * HD] > 0.5
        for half, into in ((0, keys), (1, values)):
            base = pool_ref[half, pl.ds(c * chunk_slots, chunk_slots)].reshape(chunk, HD)
            into[at, :] = jnp.where(
                is_new, new[:, half * HD : (half + 1) * HD], base.astype(jnp.float32)
            ).astype(jnp.bfloat16)

    for k in range(1, 8):
        q2(k).wait()
    queries[...] = (
        pkq[...].astype(jnp.float32).reshape(n_seq * PADDED, 2 * HD).astype(jnp.bfloat16)
    )

    def part_copy(d):
        return remote(csend.at[d], crecv.at[me], c_s.at[d], c_r.at[me], seq=d)

    block = 64

    @pl.loop(0, 8)
    def _(i):
        away = lax.div(i + 1, 2)
        b = lax.rem(z + jnp.where(lax.rem(i, 2) == 1, away, 8 - away), 8)
        at = pl.ds(pl.multiple_of(b * block, block), block)
        dests = pl.ds(b * 8, 8)
        visible = (entry_owner[...] == req_ref[at, :]) & (entry_pos[...] <= limit_ref[at, :])
        lane = lax.broadcasted_iota(jnp.int32, (block, HD), 1)
        stats = meta_ref[at, :]
        for g in range(2):
            query = queries[at, g * HD : (g + 1) * HD]
            scores = lax.dot_general(
                query, keys[...], (((1,), (1,)), ((), ())), preferred_element_type=jnp.float32
            ) * HD ** (-0.5)
            scores = jnp.where(visible, scores, NEG_FILL)
            top = jnp.max(scores, axis=1, keepdims=True)
            some = jnp.where(top > 0.5 * NEG_FILL, 1.0, 0.0)
            weights = jnp.exp(scores - top)
            total = jnp.sum(weights, axis=1, keepdims=True) * some
            part = some * jnp.dot(
                weights.astype(jnp.bfloat16), values[...], preferred_element_type=jnp.float32
            )
            csend[dests, :, g * HD : (g + 1) * HD] = part.reshape(8, PADDED, HD).astype(jnp.bfloat16)
            for j, piece in enumerate(split(top) + split(total)):
                stats = jnp.where(lane == 6 * g + j, piece, stats)
        csend[dests, :, 2 * HD : 3 * HD] = stats.reshape(8, PADDED, HD).astype(jnp.bfloat16)

        @pl.loop(0, 8)
        def _(j):
            d = b * 8 + j

            @pl.when(d != me)
            def _():
                part_copy(d).start()

    crecv[me] = csend[me]

    @pl.loop(0, n_seq)
    def _(d):
        @pl.when(d != me)
        def _():
            remote(csend.at[d], crecv.at[d], c_s.at[d], c_r.at[d], seq=d).wait()

    stats = crecv[:, :, 2 * HD : 3 * HD].astype(jnp.float32)
    came_ref[...] = stats
    mixed = []
    for g in range(2):
        def piece(j):
            return stats[:, :, j : j + 1] + stats[:, :, j + 1 : j + 2] + stats[:, :, j + 2 : j + 3]

        top = piece(6 * g)
        peak = jnp.max(top, axis=0, keepdims=True)
        rescale = jnp.exp(top - peak)
        total = jnp.sum(piece(6 * g + 3) * rescale, axis=0)
        part = crecv[:, :, g * HD : (g + 1) * HD].astype(jnp.float32)
        summed = jnp.sum(part * rescale, axis=0)
        total = jnp.where(total > 0.0, total, 1.0)
        mixed.append((summed / total).astype(jnp.bfloat16))
    attended = jnp.concatenate(mixed, axis=1)

    def sum_copy(k):
        to = lax.rem(tp + k, n_tp)
        return remote(rsend.at[to], rrecv.at[tp], r_s.at[k], r_r.at[k], tp=to)

    for i in range(n_tp):
        rsend[i] = jnp.dot(
            attended, wout_ref[:, i * width : (i + 1) * width], preferred_element_type=jnp.float32
        ).astype(jnp.bfloat16)
    for k in range(1, n_tp):
        sum_copy(k).start()
    rrecv[tp] = rsend[tp]
    for k in range(1, n_tp):
        sum_copy(k).wait()
    result = jnp.zeros((PADDED, width), jnp.float32)
    for i in range(n_tp):
        result = result + rrecv[i].astype(jnp.float32)
    out_ref[...] = result[0 : out_ref.shape[0], :].astype(jnp.bfloat16)

    @pl.loop(1, n_seq)
    def _(k):
        page_copy(k).wait()


def place_kernel(from_ref, req_ref, start_ref, arrived_ref, pool_ref, fresh_ref, out_ref):
    slots, page = pool_ref.shape[1], pool_ref.shape[2]

    @pl.loop(0, slots)
    def _(g):
        s = from_ref[g]

        @pl.when(s >= 0)
        def _():
            out_ref[0, g] = arrived_ref[s, 0]
            out_ref[1, g] = arrived_ref[s, 1]

        @pl.when(s == -1)
        def _():
            out_ref[0, g] = pool_ref[0, g]
            out_ref[1, g] = pool_ref[1, g]

        @pl.when(s < -1)
        def _():
            out_ref[0, g] = jnp.zeros((page, HD), out_ref.dtype)
            out_ref[1, g] = jnp.zeros((page, HD), out_ref.dtype)

        start = start_ref[g]

        @pl.when((start > -STEPS) & (start < page))
        def _():
            ids = lax.broadcasted_iota(jnp.int32, (page, HD), 0)
            both = [out_ref[c, g].astype(jnp.float32) for c in range(2)]
            for t in range(STEPS):
                row = req_ref[g] * STEPS + t
                block = fresh_ref[lax.div(row, 6)]
                line = lax.broadcasted_iota(jnp.int32, block.shape, 0) == lax.rem(row, 6)
                entry = jnp.sum(jnp.where(line, block, 0.0), axis=0, keepdims=True)
                for c in range(2):
                    new = entry[:, c * HD : (c + 1) * HD]
                    both[c] = jnp.where(ids == start + t, new, both[c])
            for c in range(2):
                out_ref[c, g] = both[c].astype(out_ref.dtype)


def local(tokens, norm_gain, w_query, w_key_value, w_out, kv_pool, slot_owner, slot_dest, lengths):
    seq_count = lax.axis_size("seq")
    tp_count = lax.axis_size("tp")
    my_index = lax.axis_index("seq")
    own_rows = tokens.shape[0]
    width = tokens.shape[1]
    slot_count = kv_pool.shape[1]
    page_size = kv_pool.shape[2]
    entries = slot_count * page_size
    capacity = -(-slot_count // seq_count)
    i32 = jnp.int32
    f32 = jnp.float32
    bf16 = jnp.bfloat16

    moving = slot_dest >= 0
    target_dev = jnp.where(moving, slot_dest // slot_count, -1)
    slot_ids = jnp.arange(slot_count, dtype=i32)
    same = (target_dev[None, :] == target_dev[:, None]) & (slot_ids[None, :] < slot_ids[:, None])
    send_rank = jnp.sum(same.astype(i32), axis=1)
    buffer_slot = jnp.where(moving, target_dev * capacity + send_rank, -1)
    hot = buffer_slot[None, :] == jnp.arange(seq_count * capacity, dtype=i32)[:, None]

    def picked(values):
        return jnp.sum(jnp.where(hot, values[None, :], 0), axis=1)

    pick_slot = picked(slot_ids)
    owner_req = slot_owner[:, 0]
    owner_page = slot_owner[:, 1]
    base_len = take(lengths, owner_req)

    own_index = my_index * own_rows + jnp.arange(PADDED, dtype=i32)
    own_positions = take(lengths, own_index // STEPS) + own_index % STEPS
    frequency = ROPE_BASE ** (-jnp.arange(HD // 2, dtype=f32) * 2.0 / HD)
    angles = own_positions.astype(f32)[:, None] * frequency[None, :]
    cosine, sine = jnp.cos(angles), jnp.sin(angles)
    cosine = jnp.concatenate([cosine, cosine], axis=1)
    sine = jnp.concatenate([-sine, sine], axis=1)

    rows = seq_count * PADDED
    page_shape = (seq_count, capacity, 2, page_size, HD)
    dma = pltpu.SemaphoreType.DMA
    attn_out, arrived, came, fresh = pl.pallas_call(
        block_kernel,
        out_shape=[
            jax.ShapeDtypeStruct((own_rows, width), bf16),
            jax.ShapeDtypeStruct(page_shape, bf16),
            jax.ShapeDtypeStruct((seq_count, PADDED, HD), f32),
            jax.ShapeDtypeStruct((seq_count, PADDED, 2 * HD), f32),
        ],
        in_specs=[in_smem()] + [in_vmem()] * 11,
        out_specs=[in_vmem()] * 4,
        scratch_shapes=[
            VMEM((PADDED, width), bf16),
            VMEM((entries, rows), bf16),
            VMEM((1, entries), f32),
            VMEM((1, entries), f32),
            VMEM((rows, 1), f32),
            VMEM((rows, 1), f32),
            VMEM((rows, HD), f32),
            VMEM((tp_count, PADDED, width), bf16),
            VMEM((8, 8, PADDED, 2 * HD), bf16),
            VMEM((8, 8, PADDED, 2 * HD), bf16),
            VMEM((rows, 2 * HD), bf16),
            VMEM((rows, 3 * HD), bf16),
            VMEM((entries, HD), bf16),
            VMEM((entries, HD), bf16),
            VMEM(page_shape, bf16),
            VMEM((seq_count, PADDED, 3 * HD), bf16),
            VMEM((seq_count, PADDED, 3 * HD), bf16),
            VMEM((tp_count, PADDED, width), bf16),
            VMEM((tp_count, PADDED, width), bf16),
        ]
        + [dma((8,))] * 10
        + [dma((seq_count,))] * 4
        + [dma((8,))] * 2,
        compiler_params=pltpu.CompilerParams(collective_id=0, has_side_effects=True),
        name="block",
    )(
        pick_slot,
        tokens,
        norm_gain[None, :],
        w_query,
        w_key_value,
        w_out,
        cosine,
        sine,
        kv_pool,
        slot_owner.T,
        slot_dest[None, :],
        lengths[None, :],
    )

    came = came[:, :capacity, 12:16].astype(i32).reshape(seq_count * capacity, 4)
    lands = came[None, :, 0] - 1 == slot_ids[:, None]
    landed = jnp.any(lands, axis=1)

    def landing(values):
        return jnp.sum(jnp.where(lands, values[None, :], 0), axis=1)

    from_index = jnp.where(
        landed,
        landing(jnp.arange(seq_count * capacity, dtype=i32)),
        jnp.where(moving, -2, -1),
    )
    came_req = came[:, 1]
    came_start = take(lengths, came_req) - (came[:, 2] * 128 + came[:, 3]) * page_size
    own_start = jnp.where(
        (owner_req < 0) | moving, page_size, base_len - owner_page * page_size
    )
    final_req = jnp.where(landed, landing(came_req), owner_req)
    final_start = jnp.where(landed, landing(came_start), own_start)
    kv_moved = pl.pallas_call(
        place_kernel,
        out_shape=jax.ShapeDtypeStruct(kv_pool.shape, kv_pool.dtype),
        in_specs=[in_smem()] * 3 + [in_vmem()] * 3,
        out_specs=in_vmem(),
        name="place_pages",
    )(
        from_index,
        final_req,
        final_start,
        arrived.reshape(seq_count * capacity, 2, page_size, HD),
        kv_pool,
        fresh,
    )
    return (attn_out, kv_moved)


def solution(mesh):
    in_specs = (
        P("seq", "tp"),
        P(),
        P(None, "tp"),
        P(None, None, "tp"),
        P("tp", None),
        P(None, "seq", None, "tp"),
        P("seq", None),
        P("seq"),
        P(),
    )
    out_specs = (P("seq", "tp"), P(None, "seq", None, "tp"))
    return jax.shard_map(local, mesh=mesh, in_specs=in_specs, out_specs=out_specs, check_vma=False)
```

```python
import functools

import jax
import jax.numpy as jnp
from jax import lax
from jax.experimental import pallas as pl
from jax.experimental.pallas import tpu as pltpu
from jax.sharding import PartitionSpec as P

HD = 128
STEPS = 4
PADDED = 8
ROPE_BASE = 1000000.0
NEG_FILL = -1e30
NORM_EPS = 1e-06
VMEM = pltpu.VMEM
SMEM = pltpu.SMEM


def in_vmem():
    return pl.BlockSpec(memory_space=VMEM)


def in_smem():
    return pl.BlockSpec(memory_space=SMEM)


def take(table, index):
    ids = jnp.arange(table.shape[0], dtype=jnp.int32)
    return jnp.sum(jnp.where(index[:, None] == ids[None, :], table[None, :], 0), axis=1)


MESH = pl.DeviceIdType.MESH
EARLY = 8


def remote(source, into, send_sem, recv_sem, **where):
    return pltpu.make_async_remote_copy(
        src_ref=source,
        dst_ref=into,
        send_sem=send_sem,
        recv_sem=recv_sem,
        device_id=where,
        device_id_type=MESH,
    )


def split(value):
    first = value.astype(jnp.bfloat16).astype(jnp.float32)
    rest = value - first
    second = rest.astype(jnp.bfloat16).astype(jnp.float32)
    return first, second, rest - second


def iota(shape, dim):
    return lax.broadcasted_iota(jnp.int32, shape, dim)


def ones_where(mask):
    return jnp.where(mask, 1.0, 0.0)


def prepare(
    owner_ref, dest_ref, lengths_ref, hot, entry_owner, entry_pos, req_ref, limit_ref, meta_ref,
    n_seq, slots, page, own_rows,
):
    f32, bf16 = jnp.float32, jnp.bfloat16
    rows, entries = n_seq * PADDED, slots * page
    across = (((1,), (1,)), ((), ()))
    owner = owner_ref[...].astype(f32)
    req, number = owner[0:1, :], owner[1:2, :]
    high = jnp.floor(number * (1.0 / 128))
    low = number - high * 128.0
    line = iota((HD, slots), 0)
    parts = jnp.where(line == 0, req, jnp.where(line == 1, high, jnp.where(line == 2, low, 0.0)))
    parts = parts.astype(bf16)

    spread = ones_where(
        lax.shift_right_logical(iota((slots, entries), 1), 4) == iota((slots, entries), 0)
    ).astype(bf16)
    wide = jnp.dot(parts[0:16, :], spread, preferred_element_type=f32)
    entry_owner[...] = wide[0:1, :]
    inner = (iota((1, entries), 1) & (page - 1)).astype(f32)
    entry_pos[...] = (wide[1:2, :] * 128.0 + wide[2:3, :]) * page + inner

    def row_facts(ids):
        j = ids & (PADDED - 1)
        row = lax.shift_right_logical(ids, 3) * own_rows + j
        wanted = jnp.where(j < own_rows, lax.shift_right_logical(row, 2), -2)
        return wanted.astype(f32), (row & (STEPS - 1)).astype(f32)

    lengths = lengths_ref[...].astype(f32)
    count = lengths.shape[1]
    wanted, step = row_facts(iota((rows, 1), 0))
    match = iota((rows, count), 1).astype(f32) == wanted
    req_ref[...] = wanted
    limit_ref[...] = step + jnp.sum(jnp.where(match, lengths, 0.0), axis=1, keepdims=True)
    eye = iota((count, count), 0) == iota((count, count), 1)
    length_col = jnp.sum(jnp.where(eye, lengths, 0.0), axis=1, keepdims=True)
    wanted_row, step_row = row_facts(iota((1, rows), 1))
    match = iota((count, rows), 0).astype(f32) == wanted_row
    limit_row = step_row + jnp.sum(jnp.where(match, length_col, 0.0), axis=0, keepdims=True)

    chunk = 16 * page

    @pl.loop(0, entries // chunk)
    def _(c):
        slot = lax.shift_right_logical(iota((chunk, slots), 0), 4) + c * 16
        near = ones_where(slot == iota((chunk, slots), 1)).astype(bf16)
        tall = lax.dot_general(near, parts, across, preferred_element_type=f32)
        at_inner = (iota((chunk, 1), 0) & (page - 1)).astype(f32)
        place = (tall[:, 1:2] * 128.0 + tall[:, 2:3]) * page + at_inner
        mask = (tall[:, 0:1] == wanted_row) & (place == limit_row)
        hot[pl.ds(pl.multiple_of(c * chunk, chunk), chunk), :] = ones_where(mask).astype(bf16)

    dest = dest_ref[...].astype(f32)
    device = jnp.floor((dest + 0.5) * (1.0 / slots))
    landing = dest - device * slots
    ahead, behind = iota((slots, slots), 0), iota((slots, slots), 1)
    device_col = jnp.sum(jnp.where(ahead == behind, device, 0.0), axis=1, keepdims=True)
    rank = jnp.sum(
        ones_where((device_col == device) & (ahead < behind)), axis=0, keepdims=True
    )
    place = jnp.where(dest >= 0.0, device * 2.0 + rank, -1.0)
    ids = iota((rows, slots), 0)
    j = ids & (PADDED - 1)
    wants = jnp.where(j < 2, lax.shift_right_logical(ids, 3) * 2 + j, -2).astype(f32)
    facts = jnp.where(
        line == 12,
        landing + 1.0,
        jnp.where(line == 13, req, jnp.where(line == 14, high, jnp.where(line == 15, low, 0.0))),
    )
    meta_ref[...] = lax.dot_general(
        ones_where(wants == place).astype(bf16),
        facts.astype(bf16),
        across,
        preferred_element_type=f32,
    )


def plan(stats, owner_ref, dest_ref, lengths_ref, plan_ref, n_seq, slots, page):
    f32 = jnp.float32
    rows = n_seq * PADDED
    ids = iota((rows, slots), 0)
    j = ids & (PADDED - 1)
    index = (lax.shift_right_logical(ids, 3) * 2 + j).astype(f32)
    lands = (j < 2) & (stats[:, 12:13] == (iota((rows, slots), 1) + 1).astype(f32))

    def landing(value):
        return jnp.sum(jnp.where(lands, value, 0.0), axis=0, keepdims=True)

    landed = landing(jnp.ones((rows, slots), f32)) > 0.5
    moving = dest_ref[...].astype(f32) >= 0.0
    owner = owner_ref[...].astype(f32)
    stay = jnp.where(moving, -1.0, owner[0:1, :])
    req = jnp.where(landed, landing(stats[:, 13:14]), stay)
    number = landing(stats[:, 14:15]) * 128.0 + landing(stats[:, 15:16])
    number = jnp.where(landed, number, owner[1:2, :])
    lengths = lengths_ref[...].astype(f32)
    count = lengths.shape[1]
    eye = iota((count, count), 0) == iota((count, count), 1)
    length_col = jnp.sum(jnp.where(eye, lengths, 0.0), axis=1, keepdims=True)
    match = iota((count, slots), 0).astype(f32) == req
    base = jnp.sum(jnp.where(match, length_col, 0.0), axis=0, keepdims=True)
    start = jnp.where(req >= 0.0, base - number * page, float(page))
    source = jnp.where(landed, landing(index), jnp.where(moving, -2.0, -1.0))
    line = iota((8, slots), 0)
    table = jnp.where(line == 0, source, jnp.where(line == 1, req, start))
    plan_ref[...] = table.astype(jnp.int32)


def block_kernel(
    pick_ref, tokens_ref, gain_ref, wq_hbm, wkv_hbm, wout_hbm, cos_ref, sin_ref, pool_ref,
    owner_ref, dest_ref, lengths_ref,
    out_ref, arrived_ref, plan_ref, fresh_ref,
    wq_ref, wkv_ref, wout_ref, w_sem, tsend, hot, entry_owner, entry_pos, req_ref, limit_ref, meta_ref,
    tok, pkq, pkkv, queries, fresh_all, keys, values, outgoing, csend, crecv, rsend, rrecv,
    tok_s, tok_r, q1_s, q1_r, q2_s, q2_r, k1_s, k1_r, k2_s, k2_r,
    page_s, page_r, c_s, c_r, r_s, r_r,
):
    me = lax.axis_index("seq")
    tp = lax.axis_index("tp")
    y, z = lax.rem(me, 8), lax.div(me, 8)
    n_seq, n_tp = 64, 8
    slots, page = pool_ref.shape[1], pool_ref.shape[2]

    weights_in = [
        pltpu.make_async_copy(source, into, w_sem.at[i])
        for i, (source, into) in enumerate(
            ((wq_hbm, wq_ref), (wkv_hbm, wkv_ref), (wout_hbm, wout_ref))
        )
    ]
    for copy in weights_in:
        copy.start()

    barrier = pltpu.get_barrier_semaphore()
    for k in range(1, n_tp):
        pl.semaphore_signal(
            barrier, inc=1, device_id={"tp": lax.rem(tp + k, n_tp)}, device_id_type=MESH
        )

    @pl.loop(1, n_seq)
    def _(k):
        pl.semaphore_signal(
            barrier, inc=1, device_id={"seq": lax.rem(me + k, n_seq)}, device_id_type=MESH
        )

    tsend[...] = jnp.zeros_like(tsend)
    tsend[0 : tokens_ref.shape[0], :] = tokens_ref[...]

    @pl.loop(0, n_seq)
    def _(d):
        for i in range(2):
            s = pick_ref[d * 2 + i]
            outgoing[d, i, 0] = pool_ref[0, s]
            outgoing[d, i, 1] = pool_ref[1, s]

    prepare(
        owner_ref, dest_ref, lengths_ref, hot, entry_owner, entry_pos, req_ref, limit_ref,
        meta_ref, n_seq, slots, page, tokens_ref.shape[0],
    )
    pl.semaphore_wait(barrier, n_seq - 1 + n_tp - 1)

    def token_copy(k):
        return remote(
            tsend, tok.at[tp], tok_s.at[k], tok_r.at[k], tp=lax.rem(tp + k, n_tp)
        )

    for k in range(1, n_tp):
        token_copy(k).start()
    tok[tp] = tsend[...]

    def page_copy(k):
        turn_by = lax.rem(k * 27, n_seq)
        d = lax.rem(z + lax.div(turn_by, 8), 8) * 8 + lax.rem(y + lax.rem(turn_by, 8), 8)
        return remote(outgoing.at[d], arrived_ref.at[me], page_s.at[k], page_r.at[k], seq=d)

    @pl.loop(1, 1 + EARLY)
    def _(k):
        page_copy(k).start()

    arrived_ref[me] = outgoing[me]

    for k in range(1, n_tp):
        token_copy(k).wait()

    weights_in[0].wait()
    weights_in[1].wait()
    square = jnp.zeros((PADDED, 1), jnp.float32)
    for i in range(n_tp):
        x = tok[i].astype(jnp.float32)
        square = square + jnp.sum(x * x, axis=1, keepdims=True)
    width = tok.shape[2]
    scale = lax.rsqrt(square / (n_tp * width) + NORM_EPS)
    q = jnp.zeros((PADDED, 2 * HD), jnp.float32)
    kk = jnp.zeros((PADDED, HD), jnp.float32)
    vv = jnp.zeros((PADDED, HD), jnp.float32)
    for i in range(n_tp):
        at = slice(i * width, (i + 1) * width)
        normed = (tok[i].astype(jnp.float32) * scale * gain_ref[:, at]).astype(jnp.bfloat16)
        q = q + jnp.dot(normed, wq_ref[at, :], preferred_element_type=jnp.float32)
        kk = kk + jnp.dot(normed, wkv_ref[0, at, :], preferred_element_type=jnp.float32)
        vv = vv + jnp.dot(normed, wkv_ref[1, at, :], preferred_element_type=jnp.float32)

    def turn(x):
        return x * cos_ref[...] + pltpu.roll(x, HD // 2, 1) * sin_ref[...]

    pkq[z, y, :, 0:HD] = turn(q[:, 0:HD]).astype(jnp.bfloat16)
    pkq[z, y, :, HD : 2 * HD] = turn(q[:, HD : 2 * HD]).astype(jnp.bfloat16)
    pkkv[z, y, :, 0:HD] = turn(kk).astype(jnp.bfloat16)
    pkkv[z, y, :, HD : 2 * HD] = vv.astype(jnp.bfloat16)

    def along_y(k):
        return z * 8 + lax.rem(y + k, 8)

    def along_z(k):
        return lax.rem(z + k, 8) * 8 + y

    def q1(k):
        return remote(pkq.at[z, y], pkq.at[z, y], q1_s.at[k], q1_r.at[k], seq=along_y(k))

    def k1(k):
        return remote(pkkv.at[z, y], pkkv.at[z, y], k1_s.at[k], k1_r.at[k], seq=along_z(k))

    def q2(k):
        return remote(pkq.at[z], pkq.at[z], q2_s.at[k], q2_r.at[k], seq=along_z(k))

    def k2(k):
        return remote(pkkv.at[:, y], pkkv.at[:, y], k2_s.at[k], k2_r.at[k], seq=along_y(k))

    for k in range(1, 8):
        q1(k).start()
        k1(k).start()
    for k in range(1, 8):
        q1(k).wait()
    for k in range(1, 8):
        q2(k).start()
    for k in range(1, 8):
        k1(k).wait()
    for k in range(1, 8):
        k2(k).start()

    @pl.loop(1 + EARLY, n_seq)
    def _(k):
        page_copy(k).start()

    for k in range(1, 8):
        k2(k).wait()
    fresh = pkkv[...].astype(jnp.float32).reshape(n_seq * PADDED, 2 * HD)
    fresh_ref[...] = fresh.reshape(n_seq, PADDED, 2 * HD)
    fresh_all[:, 0 : 2 * HD] = fresh.astype(jnp.bfloat16)
    fresh_all[:, 2 * HD : 3 * HD] = jnp.ones((n_seq * PADDED, HD), jnp.bfloat16)

    chunk_slots = 16
    chunk = chunk_slots * page

    @pl.loop(0, slots // chunk_slots)
    def _(c):
        at = pl.ds(pl.multiple_of(c * chunk, chunk), chunk)
        new = jnp.dot(hot[at, :], fresh_all[...], preferred_element_type=jnp.float32)
        is_new = new[:, 2 * HD : 3 * HD] > 0.5
        for half, into in ((0, keys), (1, values)):
            base = pool_ref[half, pl.ds(c * chunk_slots, chunk_slots)].reshape(chunk, HD)
            into[at, :] = jnp.where(
                is_new, new[:, half * HD : (half + 1) * HD], base.astype(jnp.float32)
            ).astype(jnp.bfloat16)

    for k in range(1, 8):
        q2(k).wait()
    queries[...] = (
        pkq[...].astype(jnp.float32).reshape(n_seq * PADDED, 2 * HD).astype(jnp.bfloat16)
    )

    def part_copy(d):
        return remote(csend.at[d], crecv.at[me], c_s.at[d], c_r.at[me], seq=d)

    block = 64

    @pl.loop(0, 8)
    def _(i):
        away = lax.div(i + 1, 2)
        b = lax.rem(z + jnp.where(lax.rem(i, 2) == 1, away, 8 - away), 8)
        at = pl.ds(pl.multiple_of(b * block, block), block)
        dests = pl.ds(b * 8, 8)
        visible = (entry_owner[...] == req_ref[at, :]) & (entry_pos[...] <= limit_ref[at, :])
        lane = lax.broadcasted_iota(jnp.int32, (block, HD), 1)
        stats = meta_ref[at, :]
        for g in range(2):
            query = queries[at, g * HD : (g + 1) * HD]
            scores = lax.dot_general(
                query, keys[...], (((1,), (1,)), ((), ())), preferred_element_type=jnp.float32
            ) * HD ** (-0.5)
            scores = jnp.where(visible, scores, NEG_FILL)
            top = jnp.max(scores, axis=1, keepdims=True)
            some = jnp.where(top > 0.5 * NEG_FILL, 1.0, 0.0)
            weights = jnp.exp(scores - top)
            total = jnp.sum(weights, axis=1, keepdims=True) * some
            part = some * jnp.dot(
                weights.astype(jnp.bfloat16), values[...], preferred_element_type=jnp.float32
            )
            csend[dests, :, g * HD : (g + 1) * HD] = part.reshape(8, PADDED, HD).astype(jnp.bfloat16)
            for j, piece in enumerate(split(top) + split(total)):
                stats = jnp.where(lane == 6 * g + j, piece, stats)
        csend[dests, :, 2 * HD : 3 * HD] = stats.reshape(8, PADDED, HD).astype(jnp.bfloat16)

        @pl.loop(0, 8)
        def _(j):
            d = b * 8 + j

            @pl.when(d != me)
            def _():
                part_copy(d).start()

    crecv[me] = csend[me]

    @pl.loop(0, n_seq)
    def _(d):
        @pl.when(d != me)
        def _():
            remote(csend.at[d], crecv.at[d], c_s.at[d], c_r.at[d], seq=d).wait()

    stats = crecv[:, :, 2 * HD : 3 * HD].astype(jnp.float32).reshape(n_seq * PADDED, HD)
    third = iota((HD, 4 * HD), 0)
    group = lax.shift_right_logical(iota((HD, 4 * HD), 1), 7)
    gather = ones_where((third >= 3 * group) & (third < 3 * group + 3)).astype(jnp.bfloat16)
    spread = jnp.dot(stats.astype(jnp.bfloat16), gather, preferred_element_type=jnp.float32)

    def facts(j):
        return spread[:, j * HD : (j + 1) * HD].reshape(n_seq, PADDED, HD)

    mixed = []
    for g in range(2):
        top = facts(2 * g)
        rescale = jnp.exp(top - jnp.max(top, axis=0, keepdims=True))
        total = jnp.sum(facts(2 * g + 1) * rescale, axis=0)
        part = crecv[:, :, g * HD : (g + 1) * HD].astype(jnp.float32)
        summed = jnp.sum(part * rescale, axis=0)
        total = jnp.where(total > 0.0, total, 1.0)
        mixed.append((summed / total).astype(jnp.bfloat16))
    attended = jnp.concatenate(mixed, axis=1)

    def sum_copy(k):
        to = lax.rem(tp + k, n_tp)
        return remote(rsend.at[to], rrecv.at[tp], r_s.at[k], r_r.at[k], tp=to)

    weights_in[2].wait()
    for i in range(n_tp):
        rsend[i] = jnp.dot(
            attended, wout_ref[:, i * width : (i + 1) * width], preferred_element_type=jnp.float32
        ).astype(jnp.bfloat16)
    for k in range(1, n_tp):
        sum_copy(k).start()
    rrecv[tp] = rsend[tp]
    for k in range(1, n_tp):
        sum_copy(k).wait()
    result = jnp.zeros((PADDED, width), jnp.float32)
    for i in range(n_tp):
        result = result + rrecv[i].astype(jnp.float32)
    out_ref[...] = result[0 : out_ref.shape[0], :].astype(jnp.bfloat16)

    plan(stats, owner_ref, dest_ref, lengths_ref, plan_ref, n_seq, slots, page)

    @pl.loop(1, n_seq)
    def _(k):
        page_copy(k).wait()


def place_kernel(plan_ref, arrived_ref, pool_ref, fresh_ref, out_ref):
    slots, page = pool_ref.shape[1], pool_ref.shape[2]

    @pl.loop(0, slots, unroll=4)
    def _(g):
        s = plan_ref[0, g]
        at = jnp.maximum(s, 0)
        where_from = jnp.full((page, HD), s, jnp.int32)
        for c in range(2):
            kept = jnp.where(where_from == -1, pool_ref[c, g].astype(jnp.float32), 0.0)
            came = arrived_ref[at, c].astype(jnp.float32)
            out_ref[c, g] = jnp.where(where_from >= 0, came, kept).astype(out_ref.dtype)

    @pl.loop(0, slots)
    def _(g):
        start = plan_ref[2, g]

        @pl.when((start > -STEPS) & (start < page))
        def _():
            ids = lax.broadcasted_iota(jnp.int32, (page, HD), 0)
            both = [out_ref[c, g].astype(jnp.float32) for c in range(2)]
            for t in range(STEPS):
                row = plan_ref[1, g] * STEPS + t
                block = fresh_ref[lax.div(row, 6)]
                line = lax.broadcasted_iota(jnp.int32, block.shape, 0) == lax.rem(row, 6)
                entry = jnp.sum(jnp.where(line, block, 0.0), axis=0, keepdims=True)
                for c in range(2):
                    new = entry[:, c * HD : (c + 1) * HD]
                    both[c] = jnp.where(ids == start + t, new, both[c])
            for c in range(2):
                out_ref[c, g] = both[c].astype(out_ref.dtype)


def local(tokens, norm_gain, w_query, w_key_value, w_out, kv_pool, slot_owner, slot_dest, lengths):
    seq_count = lax.axis_size("seq")
    tp_count = lax.axis_size("tp")
    my_index = lax.axis_index("seq")
    own_rows = tokens.shape[0]
    width = tokens.shape[1]
    slot_count = kv_pool.shape[1]
    page_size = kv_pool.shape[2]
    entries = slot_count * page_size
    capacity = -(-slot_count // seq_count)
    i32 = jnp.int32
    f32 = jnp.float32
    bf16 = jnp.bfloat16

    moving = slot_dest >= 0
    target_dev = jnp.where(moving, slot_dest // slot_count, -1)
    slot_ids = jnp.arange(slot_count, dtype=i32)
    same = (target_dev[None, :] == target_dev[:, None]) & (slot_ids[None, :] < slot_ids[:, None])
    send_rank = jnp.sum(same.astype(i32), axis=1)
    buffer_slot = jnp.where(moving, target_dev * capacity + send_rank, -1)
    hot = buffer_slot[None, :] == jnp.arange(seq_count * capacity, dtype=i32)[:, None]

    def picked(values):
        return jnp.sum(jnp.where(hot, values[None, :], 0), axis=1)

    pick_slot = picked(slot_ids)
    own_index = my_index * own_rows + jnp.arange(PADDED, dtype=i32)
    own_positions = take(lengths, own_index // STEPS) + own_index % STEPS
    frequency = ROPE_BASE ** (-jnp.arange(HD // 2, dtype=f32) * 2.0 / HD)
    angles = own_positions.astype(f32)[:, None] * frequency[None, :]
    cosine, sine = jnp.cos(angles), jnp.sin(angles)
    cosine = jnp.concatenate([cosine, cosine], axis=1)
    sine = jnp.concatenate([-sine, sine], axis=1)

    rows = seq_count * PADDED
    page_shape = (seq_count, capacity, 2, page_size, HD)
    dma = pltpu.SemaphoreType.DMA
    attn_out, arrived, plan_table, fresh = pl.pallas_call(
        block_kernel,
        out_shape=[
            jax.ShapeDtypeStruct((own_rows, width), bf16),
            jax.ShapeDtypeStruct(page_shape, bf16),
            jax.ShapeDtypeStruct((8, slot_count), i32),
            jax.ShapeDtypeStruct((seq_count, PADDED, 2 * HD), f32),
        ],
        in_specs=[in_smem()] + [in_vmem()] * 2 + [pl.BlockSpec(memory_space=pl.ANY)] * 3
        + [in_vmem()] * 6,
        out_specs=[in_vmem()] * 4,
        scratch_shapes=[
            VMEM(w_query.shape, bf16),
            VMEM(w_key_value.shape, bf16),
            VMEM(w_out.shape, bf16),
            dma((3,)),
            VMEM((PADDED, width), bf16),
            VMEM((entries, rows), bf16),
            VMEM((1, entries), f32),
            VMEM((1, entries), f32),
            VMEM((rows, 1), f32),
            VMEM((rows, 1), f32),
            VMEM((rows, HD), f32),
            VMEM((tp_count, PADDED, width), bf16),
            VMEM((8, 8, PADDED, 2 * HD), bf16),
            VMEM((8, 8, PADDED, 2 * HD), bf16),
            VMEM((rows, 2 * HD), bf16),
            VMEM((rows, 3 * HD), bf16),
            VMEM((entries, HD), bf16),
            VMEM((entries, HD), bf16),
            VMEM(page_shape, bf16),
            VMEM((seq_count, PADDED, 3 * HD), bf16),
            VMEM((seq_count, PADDED, 3 * HD), bf16),
            VMEM((tp_count, PADDED, width), bf16),
            VMEM((tp_count, PADDED, width), bf16),
        ]
        + [dma((8,))] * 10
        + [dma((seq_count,))] * 4
        + [dma((8,))] * 2,
        compiler_params=pltpu.CompilerParams(collective_id=0, has_side_effects=True),
        name="block",
    )(
        pick_slot,
        tokens,
        norm_gain[None, :],
        w_query,
        w_key_value,
        w_out,
        cosine,
        sine,
        kv_pool,
        slot_owner.T,
        slot_dest[None, :],
        lengths[None, :],
    )

    kv_moved = pl.pallas_call(
        place_kernel,
        out_shape=jax.ShapeDtypeStruct(kv_pool.shape, kv_pool.dtype),
        in_specs=[in_smem()] + [in_vmem()] * 3,
        out_specs=in_vmem(),
        name="place_pages",
    )(
        plan_table,
        arrived.reshape(seq_count * capacity, 2, page_size, HD),
        kv_pool,
        fresh,
    )
    return (attn_out, kv_moved)


def solution(mesh):
    in_specs = (
        P("seq", "tp"),
        P(),
        P(None, "tp"),
        P(None, None, "tp"),
        P("tp", None),
        P(None, "seq", None, "tp"),
        P("seq", None),
        P("seq"),
        P(),
    )
    out_specs = (P("seq", "tp"), P(None, "seq", None, "tp"))
    return jax.shard_map(local, mesh=mesh, in_specs=in_specs, out_specs=out_specs, check_vma=False)
```

```python
import functools

import jax
import jax.numpy as jnp
from jax import lax
from jax.experimental import pallas as pl
from jax.experimental.pallas import tpu as pltpu
from jax.sharding import PartitionSpec as P

HD = 128
STEPS = 4
PADDED = 8
ROPE_BASE = 1000000.0
NEG_FILL = -1e30
NORM_EPS = 1e-06
VMEM = pltpu.VMEM
SMEM = pltpu.SMEM


def in_vmem():
    return pl.BlockSpec(memory_space=VMEM)


def in_smem():
    return pl.BlockSpec(memory_space=SMEM)


def take(table, index):
    ids = jnp.arange(table.shape[0], dtype=jnp.int32)
    return jnp.sum(jnp.where(index[:, None] == ids[None, :], table[None, :], 0), axis=1)


MESH = pl.DeviceIdType.MESH
EARLY = 20


def remote(source, into, send_sem, recv_sem, **where):
    return pltpu.make_async_remote_copy(
        src_ref=source,
        dst_ref=into,
        send_sem=send_sem,
        recv_sem=recv_sem,
        device_id=where,
        device_id_type=MESH,
    )


def split(value):
    first = value.astype(jnp.bfloat16).astype(jnp.float32)
    rest = value - first
    second = rest.astype(jnp.bfloat16).astype(jnp.float32)
    return first, second, rest - second


def iota(shape, dim):
    return lax.broadcasted_iota(jnp.int32, shape, dim)


def ones_where(mask):
    return jnp.where(mask, 1.0, 0.0)


def prepare(
    owner_ref, dest_ref, lengths_ref, hot, entry_owner, entry_pos, req_ref, limit_ref, meta_ref,
    n_seq, slots, page, own_rows,
):
    f32, bf16 = jnp.float32, jnp.bfloat16
    rows, entries = n_seq * PADDED, slots * page
    across = (((1,), (1,)), ((), ()))
    owner = owner_ref[...].astype(f32)
    req, number = owner[0:1, :], owner[1:2, :]
    high = jnp.floor(number * (1.0 / 128))
    low = number - high * 128.0
    line = iota((HD, slots), 0)
    parts = jnp.where(line == 0, req, jnp.where(line == 1, high, jnp.where(line == 2, low, 0.0)))
    parts = parts.astype(bf16)

    spread = ones_where(
        lax.shift_right_logical(iota((slots, entries), 1), 4) == iota((slots, entries), 0)
    ).astype(bf16)
    wide = jnp.dot(parts[0:16, :], spread, preferred_element_type=f32)
    entry_owner[...] = wide[0:1, :]
    inner = (iota((1, entries), 1) & (page - 1)).astype(f32)
    entry_pos[...] = (wide[1:2, :] * 128.0 + wide[2:3, :]) * page + inner

    def row_facts(ids):
        j = ids & (PADDED - 1)
        row = lax.shift_right_logical(ids, 3) * own_rows + j
        wanted = jnp.where(j < own_rows, lax.shift_right_logical(row, 2), -2)
        return wanted.astype(f32), (row & (STEPS - 1)).astype(f32)

    lengths = lengths_ref[...].astype(f32)
    count = lengths.shape[1]
    wanted, step = row_facts(iota((rows, 1), 0))
    match = iota((rows, count), 1).astype(f32) == wanted
    req_ref[...] = wanted
    limit_ref[...] = step + jnp.sum(jnp.where(match, lengths, 0.0), axis=1, keepdims=True)
    eye = iota((count, count), 0) == iota((count, count), 1)
    length_col = jnp.sum(jnp.where(eye, lengths, 0.0), axis=1, keepdims=True)
    wanted_row, step_row = row_facts(iota((1, rows), 1))
    match = iota((count, rows), 0).astype(f32) == wanted_row
    limit_row = step_row + jnp.sum(jnp.where(match, length_col, 0.0), axis=0, keepdims=True)

    chunk = 16 * page

    @pl.loop(0, entries // chunk)
    def _(c):
        slot = lax.shift_right_logical(iota((chunk, slots), 0), 4) + c * 16
        near = ones_where(slot == iota((chunk, slots), 1)).astype(bf16)
        tall = lax.dot_general(near, parts, across, preferred_element_type=f32)
        at_inner = (iota((chunk, 1), 0) & (page - 1)).astype(f32)
        place = (tall[:, 1:2] * 128.0 + tall[:, 2:3]) * page + at_inner
        mask = (tall[:, 0:1] == wanted_row) & (place == limit_row)
        hot[pl.ds(pl.multiple_of(c * chunk, chunk), chunk), :] = ones_where(mask).astype(bf16)

    dest = dest_ref[...].astype(f32)
    device = jnp.floor((dest + 0.5) * (1.0 / slots))
    landing = dest - device * slots
    ahead, behind = iota((slots, slots), 0), iota((slots, slots), 1)
    device_col = jnp.sum(jnp.where(ahead == behind, device, 0.0), axis=1, keepdims=True)
    rank = jnp.sum(
        ones_where((device_col == device) & (ahead < behind)), axis=0, keepdims=True
    )
    place = jnp.where(dest >= 0.0, device * 2.0 + rank, -1.0)
    ids = iota((rows, slots), 0)
    j = ids & (PADDED - 1)
    wants = jnp.where(j < 2, lax.shift_right_logical(ids, 3) * 2 + j, -2).astype(f32)
    facts = jnp.where(
        line == 12,
        landing + 1.0,
        jnp.where(line == 13, req, jnp.where(line == 14, high, jnp.where(line == 15, low, 0.0))),
    )
    meta_ref[...] = lax.dot_general(
        ones_where(wants == place).astype(bf16),
        facts.astype(bf16),
        across,
        preferred_element_type=f32,
    )


def plan(stats, owner_ref, dest_ref, lengths_ref, plan_ref, n_seq, slots, page):
    f32 = jnp.float32
    rows = n_seq * PADDED
    ids = iota((rows, slots), 0)
    j = ids & (PADDED - 1)
    index = (lax.shift_right_logical(ids, 3) * 2 + j).astype(f32)
    lands = (j < 2) & (stats[:, 12:13] == (iota((rows, slots), 1) + 1).astype(f32))

    def landing(value):
        return jnp.sum(jnp.where(lands, value, 0.0), axis=0, keepdims=True)

    landed = landing(jnp.ones((rows, slots), f32)) > 0.5
    moving = dest_ref[...].astype(f32) >= 0.0
    owner = owner_ref[...].astype(f32)
    stay = jnp.where(moving, -1.0, owner[0:1, :])
    req = jnp.where(landed, landing(stats[:, 13:14]), stay)
    number = landing(stats[:, 14:15]) * 128.0 + landing(stats[:, 15:16])
    number = jnp.where(landed, number, owner[1:2, :])
    lengths = lengths_ref[...].astype(f32)
    count = lengths.shape[1]
    eye = iota((count, count), 0) == iota((count, count), 1)
    length_col = jnp.sum(jnp.where(eye, lengths, 0.0), axis=1, keepdims=True)
    match = iota((count, slots), 0).astype(f32) == req
    base = jnp.sum(jnp.where(match, length_col, 0.0), axis=0, keepdims=True)
    start = jnp.where(req >= 0.0, base - number * page, float(page))
    source = jnp.where(landed, landing(index), jnp.where(moving, -2.0, -1.0))
    line = iota((8, slots), 0)
    table = jnp.where(line == 0, source, jnp.where(line == 1, req, start))
    plan_ref[...] = table.astype(jnp.int32)


def block_kernel(
    pick_ref, tokens_ref, gain_ref, wq_hbm, wkv_hbm, wout_hbm, cos_ref, sin_ref, pool_ref,
    owner_ref, dest_ref, lengths_ref,
    out_ref, arrived_ref, plan_ref, fresh_ref,
    wq_ref, wkv_ref, wout_ref, w_sem, tsend, hot, entry_owner, entry_pos, req_ref, limit_ref, meta_ref,
    tok, pkq, pkkv, queries, fresh_all, keys, values, outgoing, csend, crecv, rsend, rrecv,
    tok_s, tok_r, q1_s, q1_r, q2_s, q2_r, k1_s, k1_r, k2_s, k2_r,
    page_s, page_r, c_s, c_r, r_s, r_r,
):
    me = lax.axis_index("seq")
    tp = lax.axis_index("tp")
    y, z = lax.rem(me, 8), lax.div(me, 8)
    n_seq, n_tp = 64, 8
    slots, page = pool_ref.shape[1], pool_ref.shape[2]

    weights_in = [
        pltpu.make_async_copy(source, into, w_sem.at[i])
        for i, (source, into) in enumerate(
            ((wq_hbm, wq_ref), (wkv_hbm, wkv_ref), (wout_hbm, wout_ref))
        )
    ]
    for copy in weights_in:
        copy.start()

    barrier = pltpu.get_barrier_semaphore()
    for k in range(1, n_tp):
        pl.semaphore_signal(
            barrier, inc=1, device_id={"tp": lax.rem(tp + k, n_tp)}, device_id_type=MESH
        )

    @pl.loop(1, n_seq)
    def _(k):
        pl.semaphore_signal(
            barrier, inc=1, device_id={"seq": lax.rem(me + k, n_seq)}, device_id_type=MESH
        )

    tsend[...] = jnp.zeros_like(tsend)
    tsend[0 : tokens_ref.shape[0], :] = tokens_ref[...]

    @pl.loop(0, n_seq)
    def _(d):
        for i in range(2):
            s = pick_ref[d * 2 + i]
            outgoing[d, i, 0] = pool_ref[0, s]
            outgoing[d, i, 1] = pool_ref[1, s]

    prepare(
        owner_ref, dest_ref, lengths_ref, hot, entry_owner, entry_pos, req_ref, limit_ref,
        meta_ref, n_seq, slots, page, tokens_ref.shape[0],
    )
    pl.semaphore_wait(barrier, n_seq - 1 + n_tp - 1)

    def token_copy(k):
        return remote(
            tsend, tok.at[tp], tok_s.at[k], tok_r.at[k], tp=lax.rem(tp + k, n_tp)
        )

    for k in range(1, n_tp):
        token_copy(k).start()
    tok[tp] = tsend[...]

    def page_copy(k):
        turn_by = lax.rem(k * 27, n_seq)
        d = lax.rem(z + lax.div(turn_by, 8), 8) * 8 + lax.rem(y + lax.rem(turn_by, 8), 8)
        return remote(outgoing.at[d], arrived_ref.at[me], page_s.at[k], page_r.at[k], seq=d)

    @pl.loop(1, 1 + EARLY)
    def _(k):
        page_copy(k).start()

    arrived_ref[me] = outgoing[me]

    for k in range(1, n_tp):
        token_copy(k).wait()

    weights_in[0].wait()
    weights_in[1].wait()
    square = jnp.zeros((PADDED, 1), jnp.float32)
    for i in range(n_tp):
        x = tok[i].astype(jnp.float32)
        square = square + jnp.sum(x * x, axis=1, keepdims=True)
    width = tok.shape[2]
    scale = lax.rsqrt(square / (n_tp * width) + NORM_EPS)
    q = jnp.zeros((PADDED, 2 * HD), jnp.float32)
    kk = jnp.zeros((PADDED, HD), jnp.float32)
    vv = jnp.zeros((PADDED, HD), jnp.float32)
    for i in range(n_tp):
        at = slice(i * width, (i + 1) * width)
        normed = (tok[i].astype(jnp.float32) * scale * gain_ref[:, at]).astype(jnp.bfloat16)
        q = q + jnp.dot(normed, wq_ref[at, :], preferred_element_type=jnp.float32)
        kk = kk + jnp.dot(normed, wkv_ref[0, at, :], preferred_element_type=jnp.float32)
        vv = vv + jnp.dot(normed, wkv_ref[1, at, :], preferred_element_type=jnp.float32)

    def turn(x):
        return x * cos_ref[...] + pltpu.roll(x, HD // 2, 1) * sin_ref[...]

    pkq[z, y, :, 0:HD] = turn(q[:, 0:HD]).astype(jnp.bfloat16)
    pkq[z, y, :, HD : 2 * HD] = turn(q[:, HD : 2 * HD]).astype(jnp.bfloat16)
    pkkv[z, y, :, 0:HD] = turn(kk).astype(jnp.bfloat16)
    pkkv[z, y, :, HD : 2 * HD] = vv.astype(jnp.bfloat16)

    def along_y(k):
        return z * 8 + lax.rem(y + k, 8)

    def along_z(k):
        return lax.rem(z + k, 8) * 8 + y

    def q1(k):
        return remote(pkq.at[z, y], pkq.at[z, y], q1_s.at[k], q1_r.at[k], seq=along_y(k))

    def k1(k):
        return remote(pkkv.at[z, y], pkkv.at[z, y], k1_s.at[k], k1_r.at[k], seq=along_z(k))

    def q2(k):
        return remote(pkq.at[z], pkq.at[z], q2_s.at[k], q2_r.at[k], seq=along_z(k))

    def k2(k):
        return remote(pkkv.at[:, y], pkkv.at[:, y], k2_s.at[k], k2_r.at[k], seq=along_y(k))

    for k in range(1, 8):
        q1(k).start()
        k1(k).start()
    for k in range(1, 8):
        q1(k).wait()
    for k in range(1, 8):
        q2(k).start()
    for k in range(1, 8):
        k1(k).wait()
    for k in range(1, 8):
        k2(k).start()

    @pl.loop(1 + EARLY, n_seq)
    def _(k):
        page_copy(k).start()

    for k in range(1, 8):
        k2(k).wait()
    fresh = pkkv[...].astype(jnp.float32).reshape(n_seq * PADDED, 2 * HD)
    fresh_ref[...] = fresh.reshape(n_seq, PADDED, 2 * HD)
    fresh_all[:, 0 : 2 * HD] = fresh.astype(jnp.bfloat16)
    fresh_all[:, 2 * HD : 3 * HD] = jnp.ones((n_seq * PADDED, HD), jnp.bfloat16)

    chunk_slots = 16
    chunk = chunk_slots * page

    @pl.loop(0, slots // chunk_slots)
    def _(c):
        at = pl.ds(pl.multiple_of(c * chunk, chunk), chunk)
        new = jnp.dot(hot[at, :], fresh_all[...], preferred_element_type=jnp.float32)
        is_new = new[:, 2 * HD : 3 * HD] > 0.5
        for half, into in ((0, keys), (1, values)):
            base = pool_ref[half, pl.ds(c * chunk_slots, chunk_slots)].reshape(chunk, HD)
            into[at, :] = jnp.where(
                is_new, new[:, half * HD : (half + 1) * HD], base.astype(jnp.float32)
            ).astype(jnp.bfloat16)

    for k in range(1, 8):
        q2(k).wait()
    queries[...] = (
        pkq[...].astype(jnp.float32).reshape(n_seq * PADDED, 2 * HD).astype(jnp.bfloat16)
    )

    def part_copy(d):
        return remote(csend.at[d], crecv.at[me], c_s.at[d], c_r.at[me], seq=d)

    block = 64

    @pl.loop(0, 8)
    def _(i):
        away = lax.div(i + 1, 2)
        b = lax.rem(z + jnp.where(lax.rem(i, 2) == 1, away, 8 - away), 8)
        at = pl.ds(pl.multiple_of(b * block, block), block)
        dests = pl.ds(b * 8, 8)
        visible = (entry_owner[...] == req_ref[at, :]) & (entry_pos[...] <= limit_ref[at, :])
        lane = lax.broadcasted_iota(jnp.int32, (block, HD), 1)
        stats = meta_ref[at, :]
        for g in range(2):
            query = queries[at, g * HD : (g + 1) * HD]
            scores = lax.dot_general(
                query, keys[...], (((1,), (1,)), ((), ())), preferred_element_type=jnp.float32
            ) * HD ** (-0.5)
            scores = jnp.where(visible, scores, NEG_FILL)
            top = jnp.max(scores, axis=1, keepdims=True)
            some = jnp.where(top > 0.5 * NEG_FILL, 1.0, 0.0)
            weights = jnp.exp(scores - top)
            total = jnp.sum(weights, axis=1, keepdims=True) * some
            part = some * jnp.dot(
                weights.astype(jnp.bfloat16), values[...], preferred_element_type=jnp.float32
            )
            csend[dests, :, g * HD : (g + 1) * HD] = part.reshape(8, PADDED, HD).astype(jnp.bfloat16)
            for j, piece in enumerate(split(top) + split(total)):
                stats = jnp.where(lane == 6 * g + j, piece, stats)
        csend[dests, :, 2 * HD : 3 * HD] = stats.reshape(8, PADDED, HD).astype(jnp.bfloat16)

        @pl.loop(0, 8)
        def _(j):
            d = b * 8 + j

            @pl.when(d != me)
            def _():
                part_copy(d).start()

    crecv[me] = csend[me]

    @pl.loop(0, n_seq)
    def _(d):
        @pl.when(d != me)
        def _():
            remote(csend.at[d], crecv.at[d], c_s.at[d], c_r.at[d], seq=d).wait()

    stats = crecv[:, :, 2 * HD : 3 * HD].astype(jnp.float32).reshape(n_seq * PADDED, HD)
    third = iota((HD, 4 * HD), 0)
    group = lax.shift_right_logical(iota((HD, 4 * HD), 1), 7)
    gather = ones_where((third >= 3 * group) & (third < 3 * group + 3)).astype(jnp.bfloat16)
    spread = jnp.dot(stats.astype(jnp.bfloat16), gather, preferred_element_type=jnp.float32)

    def facts(j):
        return spread[:, j * HD : (j + 1) * HD].reshape(n_seq, PADDED, HD)

    mixed = []
    for g in range(2):
        top = facts(2 * g)
        rescale = jnp.exp(top - jnp.max(top, axis=0, keepdims=True))
        total = jnp.sum(facts(2 * g + 1) * rescale, axis=0)
        part = crecv[:, :, g * HD : (g + 1) * HD].astype(jnp.float32)
        summed = jnp.sum(part * rescale, axis=0)
        total = jnp.where(total > 0.0, total, 1.0)
        mixed.append((summed / total).astype(jnp.bfloat16))
    attended = jnp.concatenate(mixed, axis=1)

    def sum_copy(k):
        to = lax.rem(tp + k, n_tp)
        return remote(rsend.at[to], rrecv.at[tp], r_s.at[k], r_r.at[k], tp=to)

    weights_in[2].wait()
    for i in range(n_tp):
        rsend[i] = jnp.dot(
            attended, wout_ref[:, i * width : (i + 1) * width], preferred_element_type=jnp.float32
        ).astype(jnp.bfloat16)
    for k in range(1, n_tp):
        sum_copy(k).start()
    rrecv[tp] = rsend[tp]
    for k in range(1, n_tp):
        sum_copy(k).wait()
    result = jnp.zeros((PADDED, width), jnp.float32)
    for i in range(n_tp):
        result = result + rrecv[i].astype(jnp.float32)
    out_ref[...] = result[0 : out_ref.shape[0], :].astype(jnp.bfloat16)

    plan(stats, owner_ref, dest_ref, lengths_ref, plan_ref, n_seq, slots, page)

    @pl.loop(1, n_seq)
    def _(k):
        page_copy(k).wait()


def place_kernel(plan_ref, arrived_ref, pool_ref, fresh_ref, out_ref):
    slots, page = pool_ref.shape[1], pool_ref.shape[2]

    @pl.loop(0, slots, unroll=4)
    def _(g):
        s = plan_ref[0, g]
        at = jnp.maximum(s, 0)
        where_from = jnp.full((page, HD), s, jnp.int32)
        for c in range(2):
            kept = jnp.where(where_from == -1, pool_ref[c, g].astype(jnp.float32), 0.0)
            came = arrived_ref[at, c].astype(jnp.float32)
            out_ref[c, g] = jnp.where(where_from >= 0, came, kept).astype(out_ref.dtype)

    @pl.loop(0, slots)
    def _(g):
        start = plan_ref[2, g]

        @pl.when((start > -STEPS) & (start < page))
        def _():
            ids = lax.broadcasted_iota(jnp.int32, (page, HD), 0)
            both = [out_ref[c, g].astype(jnp.float32) for c in range(2)]
            for t in range(STEPS):
                row = plan_ref[1, g] * STEPS + t
                block = fresh_ref[lax.div(row, 6)]
                line = lax.broadcasted_iota(jnp.int32, block.shape, 0) == lax.rem(row, 6)
                entry = jnp.sum(jnp.where(line, block, 0.0), axis=0, keepdims=True)
                for c in range(2):
                    new = entry[:, c * HD : (c + 1) * HD]
                    both[c] = jnp.where(ids == start + t, new, both[c])
            for c in range(2):
                out_ref[c, g] = both[c].astype(out_ref.dtype)


def local(tokens, norm_gain, w_query, w_key_value, w_out, kv_pool, slot_owner, slot_dest, lengths):
    seq_count = lax.axis_size("seq")
    tp_count = lax.axis_size("tp")
    my_index = lax.axis_index("seq")
    own_rows = tokens.shape[0]
    width = tokens.shape[1]
    slot_count = kv_pool.shape[1]
    page_size = kv_pool.shape[2]
    entries = slot_count * page_size
    capacity = -(-slot_count // seq_count)
    i32 = jnp.int32
    f32 = jnp.float32
    bf16 = jnp.bfloat16

    moving = slot_dest >= 0
    target_dev = jnp.where(moving, slot_dest // slot_count, -1)
    slot_ids = jnp.arange(slot_count, dtype=i32)
    same = (target_dev[None, :] == target_dev[:, None]) & (slot_ids[None, :] < slot_ids[:, None])
    send_rank = jnp.sum(same.astype(i32), axis=1)
    buffer_slot = jnp.where(moving, target_dev * capacity + send_rank, -1)
    hot = buffer_slot[None, :] == jnp.arange(seq_count * capacity, dtype=i32)[:, None]

    def picked(values):
        return jnp.sum(jnp.where(hot, values[None, :], 0), axis=1)

    pick_slot = picked(slot_ids)
    own_index = my_index * own_rows + jnp.arange(PADDED, dtype=i32)
    own_positions = take(lengths, own_index // STEPS) + own_index % STEPS
    frequency = ROPE_BASE ** (-jnp.arange(HD // 2, dtype=f32) * 2.0 / HD)
    angles = own_positions.astype(f32)[:, None] * frequency[None, :]
    cosine, sine = jnp.cos(angles), jnp.sin(angles)
    cosine = jnp.concatenate([cosine, cosine], axis=1)
    sine = jnp.concatenate([-sine, sine], axis=1)

    rows = seq_count * PADDED
    page_shape = (seq_count, capacity, 2, page_size, HD)
    dma = pltpu.SemaphoreType.DMA
    attn_out, arrived, plan_table, fresh = pl.pallas_call(
        block_kernel,
        out_shape=[
            jax.ShapeDtypeStruct((own_rows, width), bf16),
            jax.ShapeDtypeStruct(page_shape, bf16),
            jax.ShapeDtypeStruct((8, slot_count), i32),
            jax.ShapeDtypeStruct((seq_count, PADDED, 2 * HD), f32),
        ],
        in_specs=[in_smem()] + [in_vmem()] * 2 + [pl.BlockSpec(memory_space=pl.ANY)] * 3
        + [in_vmem()] * 6,
        out_specs=[in_vmem()] * 4,
        scratch_shapes=[
            VMEM(w_query.shape, bf16),
            VMEM(w_key_value.shape, bf16),
            VMEM(w_out.shape, bf16),
            dma((3,)),
            VMEM((PADDED, width), bf16),
            VMEM((entries, rows), bf16),
            VMEM((1, entries), f32),
            VMEM((1, entries), f32),
            VMEM((rows, 1), f32),
            VMEM((rows, 1), f32),
            VMEM((rows, HD), f32),
            VMEM((tp_count, PADDED, width), bf16),
            VMEM((8, 8, PADDED, 2 * HD), bf16),
            VMEM((8, 8, PADDED, 2 * HD), bf16),
            VMEM((rows, 2 * HD), bf16),
            VMEM((rows, 3 * HD), bf16),
            VMEM((entries, HD), bf16),
            VMEM((entries, HD), bf16),
            VMEM(page_shape, bf16),
            VMEM((seq_count, PADDED, 3 * HD), bf16),
            VMEM((seq_count, PADDED, 3 * HD), bf16),
            VMEM((tp_count, PADDED, width), bf16),
            VMEM((tp_count, PADDED, width), bf16),
        ]
        + [dma((8,))] * 10
        + [dma((seq_count,))] * 4
        + [dma((8,))] * 2,
        compiler_params=pltpu.CompilerParams(collective_id=0, has_side_effects=True),
        name="block",
    )(
        pick_slot,
        tokens,
        norm_gain[None, :],
        w_query,
        w_key_value,
        w_out,
        cosine,
        sine,
        kv_pool,
        slot_owner.T,
        slot_dest[None, :],
        lengths[None, :],
    )

    kv_moved = pl.pallas_call(
        place_kernel,
        out_shape=jax.ShapeDtypeStruct(kv_pool.shape, kv_pool.dtype),
        in_specs=[in_smem()] + [in_vmem()] * 3,
        out_specs=in_vmem(),
        name="place_pages",
    )(
        plan_table,
        arrived.reshape(seq_count * capacity, 2, page_size, HD),
        kv_pool,
        fresh,
    )
    return (attn_out, kv_moved)


def solution(mesh):
    in_specs = (
        P("seq", "tp"),
        P(),
        P(None, "tp"),
        P(None, None, "tp"),
        P("tp", None),
        P(None, "seq", None, "tp"),
        P("seq", None),
        P("seq"),
        P(),
    )
    out_specs = (P("seq", "tp"), P(None, "seq", None, "tp"))
    return jax.shard_map(local, mesh=mesh, in_specs=in_specs, out_specs=out_specs, check_vma=False)
```
